32 devices in a mesh: fsdp: 8 (over z, core), tp: 4 (over y, x).
Axes of the slice: x: 2, y: 2, z: 4, core: 2. Of those that a mesh axis runs over, the one named last changes fastest.
Arguments:
- tokens_in: bfloat16 [16384, 1536], P(('fsdp', 'tp')), may hold values from -6 to 6
- cotangent: bfloat16 [16384, 1536], P(('fsdp', 'tp')), may hold values from -6 to 6
- piece_starts: int32 [16, 2], P('fsdp'), may hold values from 0 to 768, as said below
- adapter_ids: int32 [16], P('fsdp'), may hold values from 0 to 7, as said below
- gain_att: bfloat16 [1, 1536], P(None, ('fsdp', 'tp')), may hold values from 0.5 to 1.5
- w_in: bfloat16 [1, 1536, 4, 1536], P(None, 'fsdp', None, 'tp'), may hold values from -0.15625 to 0.15625
- w_forget: bfloat16 [1, 1536, 24], P(None, 'fsdp', 'tp'), may hold values from -0.078125 to 0.078125
- bias_forget: bfloat16 [1, 24], P(None, 'tp'), may hold values from 2.5 to 8
- w_out: bfloat16 [1, 1536, 1536], P(None, 'tp', 'fsdp'), may hold values from -0.625 to 0.625
- gain_mlp: bfloat16 [1, 1536], P(None, ('fsdp', 'tp')), may hold values from 0.5 to 1.5
- w_gate_up: bfloat16 [1, 1536, 2, 4096], P(None, 'fsdp', None, 'tp'), may hold values from -0.15625 to 0.15625
- w_down: bfloat16 [1, 4096, 1536], P(None, 'tp', 'fsdp'), may hold values from -0.1875 to 0.1875
- adapt_in_a: bfloat16 [1, 1536, 640], P(None, ('fsdp', 'tp')), may hold values from -0.15625 to 0.15625
- adapt_in_b: bfloat16 [1, 4, 128, 1536], P(None, None, 'fsdp', 'tp'), may hold values from -1.5 to 1.5
- adapt_forget_b: bfloat16 [1, 128, 24], P(None, 'fsdp', 'tp'), may hold values from -0.75 to 0.75
- adapt_out_a: bfloat16 [1, 1536, 128], P(None, 'tp', 'fsdp'), may hold values from -0.625 to 0.625
- adapt_out_b: bfloat16 [1, 128, 1536], P(None, None, ('fsdp', 'tp')), may hold values from -1.5 to 1.5
- adapt_mlp_a: bfloat16 [1, 1536, 256], P(None, ('fsdp', 'tp')), may hold values from -0.15625 to 0.15625
- adapt_gu_b: bfloat16 [1, 2, 128, 4096], P(None, None, 'fsdp', 'tp'), may hold values from -1.5 to 1.5
- adapt_down_a: bfloat16 [1, 4096, 128], P(None, 'tp', 'fsdp'), may hold values from -0.1875 to 0.1875
- adapt_down_b: bfloat16 [1, 128, 1536], P(None, None, ('fsdp', 'tp')), may hold values from -1.5 to 1.5
Outputs:
- activations: bfloat16 [16384, 1536], P(('fsdp', 'tp'))
- input_grad: float32 [16384, 1536], P(('fsdp', 'tp'))
- grad_in_a: float32 [1, 1536, 640], P(None, ('fsdp', 'tp'))
- grad_in_b: float32 [1, 4, 128, 1536], P(None, None, 'fsdp', 'tp')
- grad_forget_b: float32 [1, 128, 24], P(None, 'fsdp', 'tp')
- grad_out_a: float32 [1, 1536, 128], P(None, 'tp', 'fsdp')
- grad_out_b: float32 [1, 128, 1536], P(None, None, ('fsdp', 'tp'))
- grad_mlp_a: float32 [1, 1536, 256], P(None, ('fsdp', 'tp'))
- grad_gu_b: float32 [1, 2, 128, 4096], P(None, None, 'fsdp', 'tp')
- grad_down_a: float32 [1, 4096, 128], P(None, 'tp', 'fsdp')
- grad_down_b: float32 [1, 128, 1536], P(None, None, ('fsdp', 'tp'))
The draws below stay inside these ranges and needn't reach their ends.
Inputs may be any that keep to these rules, and one draw needn't show every extreme that they name: `piece_starts`: each sequence has 2 picture pieces of 256 positions, given by their first positions in increasing order; they do not intersect and lie inside the sequence. `adapter_ids`: every one of the 8 adapters is used by some sequence.
All inputs are finite; a program needn't handle non-finite values.
Results may differ from the reference program's by a relative error of at most 0.023.
Values may be sent and summed in bfloat16 or wider, within the bound.
No kernel may reach another device: no remote copies, remote signals or barrier semaphores. Data moves between devices by JAX's collectives and lax.ppermute only.
A program may use at most 256 MiB of HBM per device.

```python
import jax
import jax.numpy as jnp
from jax import lax

D = 1536
HEADS = 24
HEAD = 64
FF = 4096
RANK = 16
ADAPTERS = 8
PIECE = 256
PIECES = 2
LEN = 1024
LAYERS = 1
SEQS = 2
SEQUENCES = 16
TOKENS = 16384
N_FSDP = 8


def draw_piece_starts(key, part):
    text_len = LEN - PIECES * PIECE
    split_a, split_b = jax.random.split(jax.random.fold_in(key, 11))
    cut_first = jax.random.randint(split_a, (SEQUENCES,), 0, text_len + 1)
    cut_second = jax.random.randint(split_b, (SEQUENCES,), 0, text_len + 1)
    low_cut = jnp.minimum(cut_first, cut_second)
    high_cut = jnp.maximum(cut_first, cut_second)
    seq_index = jnp.arange(SEQUENCES)
    low_cut = jnp.where(seq_index == 1, 0, low_cut)
    high_cut = jnp.where(seq_index == 0, text_len, high_cut)
    high_cut = jnp.maximum(high_cut, low_cut)
    return jnp.stack([low_cut, high_cut + PIECE], axis=1).astype(jnp.int32)


def draw_adapter_ids(key, part):
    split_a, split_b = jax.random.split(jax.random.fold_in(key, 7))
    rank_order = jax.random.permutation(split_a, SEQUENCES)
    fill_ids = jax.random.randint(split_b, (SEQUENCES,), 0, ADAPTERS)
    return jnp.where(rank_order < ADAPTERS, rank_order, fill_ids).astype(jnp.int32)


def block_scale(rng, shape, pieces, least, high):
    def one(axis_at, parts):
        steps = jax.random.uniform(jax.random.fold_in(jax.random.fold_in(rng, 6), axis_at), (parts,), jnp.float32, least / len(pieces), high / len(pieces))
        return jnp.repeat(jnp.exp(steps), shape[axis_at] // parts).reshape((-1,) + (1,) * (len(shape) - axis_at - 1))

    factor_of = one(*pieces[0])
    for cut in pieces[1:]:
        factor_of = factor_of * one(*cut)
    return factor_of


def bell_draw(key, dims, width, bound, shards=(), dtype=jnp.bfloat16):
    array = width * jax.random.normal(key, dims, jnp.float32)
    if shards:
        array = array * block_scale(key, dims, shards, -0.22, 0.18)
    return jnp.clip(array, -bound, bound).astype(dtype)


def setup_inputs(seed: int = 0) -> dict:
    key_list = jax.random.split(jax.random.key(seed), 22)
    tokens_in = bell_draw(key_list[0], (TOKENS, D), 1.0, 6.0, ((0, 32),))
    cotangent = bell_draw(key_list[1], (TOKENS, D), 1.0, 6.0, ((0, 32),))
    piece_starts = draw_piece_starts(jax.random.fold_in(key_list[21], 71), 0)
    adapter_ids = draw_adapter_ids(jax.random.fold_in(key_list[21], 71), 0)
    gain_att = jnp.clip(1.0 + 0.1 * jax.random.normal(key_list[4], (LAYERS, D), jnp.float32), 0.5, 1.5).astype(jnp.bfloat16)
    w_in = bell_draw(key_list[5], (LAYERS, D, 4, D), D ** -0.5, 0.15625, ((1, 8), (3, 4)))
    w_forget = bell_draw(key_list[6], (LAYERS, D, HEADS), (4 * D) ** -0.5, 0.078125, ((1, 8), (2, 4)))
    bias_forget = jnp.clip(2.5 + 5.5 * jax.random.uniform(key_list[7], (LAYERS, HEADS), jnp.float32) ** block_scale(key_list[7], (LAYERS, HEADS), ((1, 4),), -0.2, 0.2), 2.5, 8.0).astype(jnp.bfloat16)
    w_out = bell_draw(key_list[8], (LAYERS, D, D), (D // 16) ** -0.5, 0.625, ((1, 4), (2, 8)))
    gain_mlp = jnp.clip(1.0 + 0.1 * jax.random.normal(key_list[9], (LAYERS, D), jnp.float32), 0.5, 1.5).astype(jnp.bfloat16)
    w_gate_up = bell_draw(key_list[10], (LAYERS, D, 2, FF), D ** -0.5, 0.15625, ((1, 8), (3, 4)))
    w_down = bell_draw(key_list[11], (LAYERS, FF, D), (FF // 4) ** -0.5, 0.1875, ((1, 4), (2, 8)))
    adapt_in_a = bell_draw(key_list[12], (LAYERS, D, 5 * ADAPTERS * RANK), D ** -0.5, 0.15625, ((1, 32),))
    adapt_in_b = bell_draw(key_list[13], (LAYERS, 4, ADAPTERS * RANK, D), RANK ** -0.5, 1.5, ((2, 8), (3, 4)))
    adapt_forget_b = bell_draw(key_list[14], (LAYERS, ADAPTERS * RANK, HEADS), (4 * RANK) ** -0.5, 0.75, ((1, 8), (2, 4)))
    adapt_out_a = bell_draw(key_list[15], (LAYERS, D, ADAPTERS * RANK), (D // 16) ** -0.5, 0.625, ((1, 4), (2, 8)))
    adapt_out_b = bell_draw(key_list[16], (LAYERS, ADAPTERS * RANK, D), RANK ** -0.5, 1.5, ((2, 32),))
    adapt_mlp_a = bell_draw(key_list[17], (LAYERS, D, 2 * ADAPTERS * RANK), D ** -0.5, 0.15625, ((1, 32),))
    adapt_gu_b = bell_draw(key_list[18], (LAYERS, 2, ADAPTERS * RANK, FF), RANK ** -0.5, 1.5, ((2, 8), (3, 4)))
    adapt_down_a = bell_draw(key_list[19], (LAYERS, FF, ADAPTERS * RANK), (FF // 4) ** -0.5, 0.1875, ((1, 4), (2, 8)))
    adapt_down_b = bell_draw(key_list[20], (LAYERS, ADAPTERS * RANK, D), RANK ** -0.5, 1.5, ((2, 32),))
    return dict(tokens_in=tokens_in, cotangent=cotangent, piece_starts=piece_starts, adapter_ids=adapter_ids, gain_att=gain_att, w_in=w_in, w_forget=w_forget, bias_forget=bias_forget, w_out=w_out, gain_mlp=gain_mlp, w_gate_up=w_gate_up, w_down=w_down, adapt_in_a=adapt_in_a, adapt_in_b=adapt_in_b, adapt_forget_b=adapt_forget_b, adapt_out_a=adapt_out_a, adapt_out_b=adapt_out_b, adapt_mlp_a=adapt_mlp_a, adapt_gu_b=adapt_gu_b, adapt_down_a=adapt_down_a, adapt_down_b=adapt_down_b)


epsilon = 1e-06
masked_score = -1e+30
highest = lax.Precision.HIGHEST

@jax.custom_vjp
def low(v):
    return lax.optimization_barrier(v.astype(jnp.bfloat16)).astype(jnp.float32)

@jax.custom_vjp
def low_back(v):
    return v

def low_keep(v):
    return (low(v), None)

def low_pass(kept, grad):
    return (grad,)

def back_keep(v):
    return (v, None)

def back_low(kept, grad):
    return (low(grad),)
low.defvjp(low_keep, low_pass)
low_back.defvjp(back_keep, back_low)

def matmul_hi(left, right):
    return jnp.dot(left, right, precision=highest)

def rms_norm(hidden, gain_vec):
    return hidden * lax.rsqrt(lax.optimization_barrier(jnp.mean(hidden * hidden, axis=-1, keepdims=True)) + epsilon) * gain_vec

def log_gate(logits):
    return -jnp.log1p(jnp.exp(-logits))

def allowed_pairs(starts):
    positions = jnp.arange(LEN).astype(jnp.int32)
    inside = (positions[:, None] >= starts[None, :]) & (positions[:, None] < starts[None, :] + PIECE)
    labels = lax.optimization_barrier(jnp.sum(inside.astype(jnp.int32) * (jnp.arange(PIECES).astype(jnp.int32)[None, :] + 1), axis=1))
    return (positions[None, :] <= positions[:, None]) | (labels[:, None] == labels[None, :]) & (labels[:, None] > 0)

def decay_terms(cum_log):
    positions = jnp.arange(LEN)
    earlier = positions[None, :] <= positions[:, None]
    return jnp.where(earlier[None], cum_log[:, :, None] - cum_log[:, None, :], cum_log[:, None, :] - cum_log[:, :, None])

def attend_one(packed):
    queries, key_rows, values, cum_log, allowed = packed
    scores = jnp.einsum('ihd,jhd->hij', queries, key_rows, precision=highest) * HEAD ** (-0.5)
    scores = low_back(scores + decay_terms(cum_log.T))
    scores = jnp.where(allowed[None], scores, masked_score)
    row_max = lax.optimization_barrier(jnp.max(scores, axis=-1, keepdims=True))
    weights = jnp.exp(scores - row_max)
    probs = low(weights / lax.optimization_barrier(jnp.sum(weights, axis=-1, keepdims=True)))
    return jnp.einsum('hij,jhd->ihd', probs, values, precision=highest)

def by_sequence(values_in):
    return values_in.reshape(-1, LEN, HEADS, HEAD)

def block_forward(hidden, adapters, frozen, mask_one, allowed):
    gain_att, w_in, w_forget, bias_forget, w_out, gain_mlp, w_gate_up, w_down = frozen
    adapt_in_a, adapt_in_b, adapt_forget_b, adapt_out_a, adapt_out_b, adapt_mlp_a, adapt_gu_b, adapt_down_a, adapt_down_b = adapters
    mask_two = jnp.concatenate([mask_one] * 2, axis=1)
    mask_five = jnp.concatenate([mask_one] * 5, axis=1)
    row_count = hidden.shape[0]
    adapter_width = ADAPTERS * RANK
    for layer_index in range(LAYERS):
        normed = low(rms_norm(hidden, gain_att[layer_index]))
        low_parts = (low(low_back(matmul_hi(normed, adapt_in_a[layer_index]))) * mask_five).reshape(row_count, 5, adapter_width)
        projected = jnp.einsum('td,dkh->tkh', normed, w_in[layer_index], precision=highest)
        projected = projected + jnp.einsum('tkr,krh->tkh', low_parts[:, :4], adapt_in_b[layer_index], precision=highest)
        forget_logits = low_back(matmul_hi(normed, w_forget[layer_index]) + matmul_hi(low_parts[:, 4], adapt_forget_b[layer_index]) + bias_forget[layer_index])
        queries = low(low_back(projected[:, 0]))
        key_rows = low(low_back(projected[:, 1]))
        values = low(low_back(projected[:, 2]))
        out_gate = jax.nn.sigmoid(low_back(projected[:, 3]))
        cum_log = jnp.cumsum(log_gate(forget_logits).reshape(-1, LEN, HEADS), axis=1)
        mixed_out = lax.map(jax.checkpoint(attend_one), (by_sequence(queries), by_sequence(key_rows), by_sequence(values), cum_log, allowed))
        mixed_out = low_back(mixed_out.reshape(row_count, D))
        merged = low(mixed_out * out_gate)
        low_out = low(low_back(matmul_hi(merged, adapt_out_a[layer_index]))) * mask_one
        hidden = hidden + low_back(matmul_hi(merged, w_out[layer_index]) + matmul_hi(low_out, adapt_out_b[layer_index]))
        normed = low(rms_norm(hidden, gain_mlp[layer_index]))
        low_parts = (low(low_back(matmul_hi(normed, adapt_mlp_a[layer_index]))) * mask_two).reshape(row_count, 2, adapter_width)
        pre_act = jnp.einsum('td,dkf->tkf', normed, w_gate_up[layer_index], precision=highest)
        pre_act = low_back(pre_act + jnp.einsum('tkr,krf->tkf', low_parts, adapt_gu_b[layer_index], precision=highest))
        gate_pre = pre_act[:, 0]
        inner_act = low(gate_pre * jax.nn.sigmoid(gate_pre) * pre_act[:, 1])
        low_out = low(low_back(matmul_hi(inner_act, adapt_down_a[layer_index]))) * mask_one
        hidden = hidden + low_back(matmul_hi(inner_act, w_down[layer_index]) + matmul_hi(low_out, adapt_down_b[layer_index]))
    return hidden

def reference(tokens_in, cotangent, piece_starts, adapter_ids, gain_att, w_in, w_forget, bias_forget, w_out, gain_mlp, w_gate_up, w_down, adapt_in_a, adapt_in_b, adapt_forget_b, adapt_out_a, adapt_out_b, adapt_mlp_a, adapt_gu_b, adapt_down_a, adapt_down_b):
    frozen = tuple((array_in.astype(jnp.float32) for array_in in (gain_att, w_in, w_forget, bias_forget, w_out, gain_mlp, w_gate_up, w_down)))
    adapters = tuple((array_in.astype(jnp.float32) for array_in in (adapt_in_a, adapt_in_b, adapt_forget_b, adapt_out_a, adapt_out_b, adapt_mlp_a, adapt_gu_b, adapt_down_a, adapt_down_b)))
    group_rows = SEQS * LEN
    adapter_width = ADAPTERS * RANK

    def group_step(totals, packed):
        rows_in, cot_rows, starts, seq_ids = packed
        seq_index = (jnp.arange(group_rows) // LEN).astype(jnp.int32)
        token_ids = seq_ids[seq_index]
        mask_one = ((jnp.arange(adapter_width) // RANK)[None, :] == token_ids[:, None]).astype(jnp.float32)
        allowed = jax.vmap(allowed_pairs)(starts)

        def forward(hidden, adapter_set):
            return block_forward(hidden, adapter_set, frozen, mask_one, allowed)
        result, pullback = jax.vjp(forward, rows_in.astype(jnp.float32), adapters)
        grad_rows, grad_set = pullback(cot_rows.astype(jnp.float32))
        totals = jax.tree.map(jnp.add, totals, grad_set)
        return (totals, (result.astype(jnp.bfloat16), grad_rows))
    zeros = jax.tree.map(jnp.zeros_like, adapters)
    packs = (tokens_in.reshape(N_FSDP, group_rows, D), cotangent.reshape(N_FSDP, group_rows, D), piece_starts.reshape(N_FSDP, SEQS, PIECES), adapter_ids.reshape(N_FSDP, SEQS))
    totals, (result, grad_rows) = lax.scan(group_step, zeros, packs)
    return (result.reshape(-1, D), grad_rows.reshape(-1, D), totals[0], totals[1], totals[2], totals[3], totals[4], totals[5], totals[6], totals[7], totals[8])
```

```python
import functools

import jax
import jax.numpy as jnp
from jax import lax
from jax.experimental import pallas as pl
from jax.experimental.pallas import tpu as pltpu
from jax.sharding import Mesh, PartitionSpec as P

HEAD = 64
RANK = 16
PIECE = 256
PIECES = 2
LEN = 1024
epsilon = 1e-06
masked_score = -1e30
LANES = 128
BLOCK = 256
VMEM_LIMIT = 60 * 1024 * 1024

f32 = jnp.float32
bf16 = jnp.bfloat16
ANY = pl.BlockSpec(memory_space=pl.ANY)
WHOLE = pl.BlockSpec(memory_space=pltpu.VMEM)


def mm(left, right, dims):
    return lax.dot_general(left, right, ((dims[0], dims[1]), ((), ())), preferred_element_type=f32)


def shift(value, axis, size, step):
    return lax.ppermute(value, axis, [(i, (i + step) % size) for i in range(size)])


def split3(value):
    high = value.astype(bf16)
    rest = value - high.astype(f32)
    mid = rest.astype(bf16)
    low = (rest - mid.astype(f32)).astype(bf16)
    return high, mid, low


def split_columns(value):
    high = lax.reduce_precision(value, 8, 7)
    mid = lax.reduce_precision(value - high, 8, 7)
    return jnp.concatenate([high, mid, value - high - mid], 1).astype(bf16)


def in_order(pieces, index, size):
    if size == 1:
        return pieces[0]
    if size == 2:
        return jnp.where(
            index == 0, jnp.concatenate(pieces, 0), jnp.concatenate(pieces[::-1], 0)
        )
    rows = pieces[0].shape[0]
    out = jnp.zeros((size * rows,) + pieces[0].shape[1:], pieces[0].dtype)
    for d, piece in enumerate(pieces):
        out = lax.dynamic_update_slice_in_dim(out, piece, ((index - d) % size) * rows, 0)
    return out


def assemble_kernel(count, axis, width, at_ref, *refs):
    pieces, out, buf, sem = refs[:count], refs[count], refs[count + 1], refs[count + 2]
    copies = []
    for d in range(count):
        where = pl.multiple_of(lax.rem(at_ref[0] - d + count, count) * width, width)
        spot = (slice(None),) * axis + (pl.ds(where, width),)
        copies.append(pltpu.make_async_copy(pieces[d], buf.at[spot], sem.at[d]))
    for copy in copies:
        copy.start()
    for copy in copies:
        copy.wait()
    last = pltpu.make_async_copy(buf, out, sem.at[count])
    last.start()
    last.wait()


def assemble(pieces, index, axis):
    count = len(pieces)
    shape = list(pieces[0].shape)
    width = shape[axis]
    shape[axis] = width * count
    size = 2 * functools.reduce(lambda a, b: a * b, shape)
    return pl.pallas_call(
        functools.partial(assemble_kernel, count, axis, width),
        out_shape=jax.ShapeDtypeStruct(tuple(shape), pieces[0].dtype),
        grid_spec=pltpu.PrefetchScalarGridSpec(
            num_scalar_prefetch=1,
            grid=(1,),
            in_specs=[ANY] * count,
            out_specs=ANY,
            scratch_shapes=[
                pltpu.VMEM(tuple(shape), pieces[0].dtype),
                pltpu.SemaphoreType.DMA((count + 1,)),
            ],
        ),
        cost_estimate=pl.CostEstimate(flops=0, bytes_accessed=2 * size, transcendentals=0),
        compiler_params=pltpu.CompilerParams(vmem_limit_bytes=VMEM_LIMIT),
        name="assemble",
    )(jnp.reshape(index, (1,)).astype(jnp.int32), *pieces)


def out_weight_kernel(blocks, cols, at_ref, *refs):
    mine, other = refs[:blocks], refs[blocks : 2 * blocks]
    out, buf, sem = refs[2 * blocks :]
    core = at_ref[0]
    copies = []
    for i in range(blocks):
        for k, source in enumerate((mine[i], other[i])):
            spot = buf.at[:, lax.rem(core + k, 2), :, pl.ds(i * cols, cols)]
            copies.append(pltpu.make_async_copy(source, spot, sem.at[2 * i + k]))
    for copy in copies:
        copy.start()
    for copy in copies:
        copy.wait()
    last = pltpu.make_async_copy(buf, out, sem.at[2 * blocks])
    last.start()
    last.wait()


def out_weight(mine, other, core):
    blocks = len(mine)
    nz, rows, cols = mine[0].shape
    if cols % LANES:
        mine, other = jnp.concatenate(mine, 2), jnp.concatenate(other, 2)
        return jnp.where(core == 0, jnp.stack([mine, other], 1), jnp.stack([other, mine], 1))
    shape = (nz, 2, rows, blocks * cols)
    size = 2 * nz * 2 * rows * blocks * cols
    return pl.pallas_call(
        functools.partial(out_weight_kernel, blocks, cols),
        out_shape=jax.ShapeDtypeStruct(shape, bf16),
        grid_spec=pltpu.PrefetchScalarGridSpec(
            num_scalar_prefetch=1,
            grid=(1,),
            in_specs=[ANY] * (2 * blocks),
            out_specs=ANY,
            scratch_shapes=[
                pltpu.VMEM(shape, bf16),
                pltpu.SemaphoreType.DMA((2 * blocks + 1,)),
            ],
        ),
        cost_estimate=pl.CostEstimate(flops=0, bytes_accessed=2 * size, transcendentals=0),
        compiler_params=pltpu.CompilerParams(vmem_limit_bytes=VMEM_LIMIT),
        name="out_weight",
    )(jnp.reshape(core, (1,)).astype(jnp.int32), *mine, *other)


def mlp_kernel(units, first, width, *refs):
    own, oth = refs[:units], refs[units : 2 * units]
    refs = refs[2 * units :]
    xm_ref, gz_ref, low_ref, bu_ref = refs[:4]
    refs = refs[4:]
    if not first:
        prior, refs = refs[:3], refs[3:]
    out_ref, dx_ref, small_ref, grad_ref, wbuf, sem = refs
    for u in range(units):
        for half, source in enumerate((own[u], oth[u])):
            pltpu.make_async_copy(
                source, wbuf.at[u, :, :, pl.ds(half * width, width)], sem.at[u, half]
            ).start()
    if first:
        out_ref[...] = jnp.zeros_like(out_ref)
        dx_ref[...] = jnp.zeros_like(dx_ref)
        small_ref[...] = jnp.zeros_like(small_ref)
    else:
        out_ref[...] = prior[0][...]
        dx_ref[...] = prior[1][...]
        small_ref[...] = prior[2][...]
    low_all = low_ref[...]
    lane = lax.broadcasted_iota(jnp.int32, low_all.shape, 1) // RANK
    zero = jnp.zeros_like(low_all)
    low_e, low_u, low_d = (jnp.where(lane == i, low_all, zero) for i in range(3))

    def step(u, carry):
        for half in range(2):
            spot = wbuf.at[u, :, :, pl.ds(half * width, width)]
            pltpu.make_async_copy(spot, spot, sem.at[u, half]).wait()
        bu = bu_ref[u]
        gate = mm(xm_ref[...], wbuf[u, 0], ((1,), (0,))) + mm(low_e, bu, ((1,), (0,)))
        up = mm(xm_ref[...], wbuf[u, 1], ((1,), (0,))) + mm(low_u, bu, ((1,), (0,)))
        dh = mm(gz_ref[...], wbuf[u, 2], ((1,), (0,))) + mm(low_d, bu, ((1,), (0,)))
        sig = jax.nn.sigmoid(gate)
        act = gate * sig
        inner = (act * up).astype(bf16)
        dgate = (dh * up * sig * (1.0 + gate * (1.0 - sig))).astype(bf16)
        dup = (dh * act).astype(bf16)
        out_ref[...] += mm(inner, wbuf[u, 2], ((1,), (1,)))
        dx_ref[...] += mm(dgate, wbuf[u, 0], ((1,), (1,))) + mm(dup, wbuf[u, 1], ((1,), (1,)))
        s_e = mm(dgate, bu, ((1,), (1,)))
        s_u = mm(dup, bu, ((1,), (1,)))
        s_d = mm(inner, bu, ((1,), (1,)))
        small_ref[...] += jnp.where(lane == 0, s_e, jnp.where(lane == 1, s_u, s_d))
        grad_ref[u] = (
            mm(low_e, dgate, ((0,), (0,)))
            + mm(low_u, dup, ((0,), (0,)))
            + mm(low_d, inner, ((0,), (0,)))
        ).astype(bf16)
        return carry

    lax.fori_loop(0, units, step, 0)


def mlp_call(own, oth, xm, gz, low, bu, prior):
    units = len(own)
    three, depth, width = own[0].shape
    rows = xm.shape[0]
    first = prior is None
    lanes = low.shape[1]
    flops = units * 2 * rows * depth * 2 * width * 6
    return pl.pallas_call(
        functools.partial(mlp_kernel, units, first, width),
        out_shape=(
            jax.ShapeDtypeStruct((rows, depth), f32),
            jax.ShapeDtypeStruct((rows, depth), f32),
            jax.ShapeDtypeStruct((rows, lanes), f32),
            jax.ShapeDtypeStruct((units, lanes, 2 * width), bf16),
        ),
        in_specs=[ANY] * (2 * units) + [WHOLE] * (4 + (0 if first else 3)),
        out_specs=(WHOLE,) * 4,
        scratch_shapes=[
            pltpu.VMEM((units, three, depth, 2 * width), bf16),
            pltpu.SemaphoreType.DMA((units, 2)),
        ],
        cost_estimate=pl.CostEstimate(
            flops=flops,
            bytes_accessed=units * 3 * depth * 2 * width * 2 + rows * depth * 20,
            transcendentals=units * rows * 2 * width,
        ),
        compiler_params=pltpu.CompilerParams(vmem_limit_bytes=VMEM_LIMIT),
        name="feed_forward",
    )(*own, *oth, xm, gz, low, bu, *(() if first else prior))


def decay_lanes(cum, negate):
    high, mid, low = (part.astype(f32) for part in split3(cum))
    lane = lax.broadcasted_iota(jnp.int32, cum.shape, 1) % HEAD
    one = jnp.ones_like(cum)
    if negate:
        picks = (-high, -mid, -low, one, one, one)
    else:
        picks = (one, one, one, high, mid, low)
    out = jnp.zeros_like(cum)
    for i, pick in enumerate(picks):
        out = jnp.where(lane == i, pick, out)
    return out.astype(bf16)


def pair_masks(row, col, starts):
    def label(position, none):
        out = jnp.full(position.shape, none, jnp.int32)
        for i in range(PIECES):
            inside = (position >= starts[i]) & (position < starts[i] + PIECE)
            out = jnp.where(inside, i + 1, out)
        return out

    lower = col <= row
    return lower, lower | (label(row, -1) == label(col, -2))


def hi_fix(scores, decay, lower, allowed):
    return jnp.where(lower, scores, jnp.where(allowed, scores - 2.0 * decay, masked_score))


def block_ranges(i, rows, length):
    low = i * rows
    return low, min(low + rows + PIECE, length)


def attend_kernel(length, starts_ref, q_ref, k_ref, v_ref, gate_ref, cum_ref, y_ref, o_ref, lse_ref, keys):
    starts = [starts_ref[i] for i in range(PIECES)]
    cum = cum_ref[...]
    keys[:, :LANES] = k_ref[0]
    keys[:, LANES:] = decay_lanes(cum, True)
    values = v_ref[0].astype(bf16)
    for i in range(length // BLOCK):
        low, top = block_ranges(i, BLOCK, length)
        rows = slice(low, low + BLOCK)
        lane = lax.broadcasted_iota(jnp.int32, (BLOCK, LANES), 1)
        queries = q_ref[0, rows, :] * jnp.asarray(HEAD**-0.5, bf16)
        aug = decay_lanes(cum_ref[rows, :], False)
        row = low + lax.broadcasted_iota(jnp.int32, (BLOCK, 1), 0)
        col = low + lax.broadcasted_iota(jnp.int32, (1, top - low), 1)
        lower, allowed = pair_masks(row, col, starts)
        mixed, lse = [], []
        for h in range(2):
            mine = (lane // HEAD) == h
            zero = jnp.zeros_like(queries)
            aug_h = jnp.where(mine, aug, zero)
            left = jnp.concatenate([jnp.where(mine, queries, zero), aug_h], 1)
            s_hi = mm(left, keys[low:top, :], ((1,), (1,)))
            decay = mm(aug_h, keys[low:top, LANES:], ((1,), (1,)))
            s_hi = hi_fix(s_hi, decay, lower, allowed)
            top_score = jnp.max(s_hi, axis=1, keepdims=True)
            if low:
                s_lo = mm(left, keys[:low, :], ((1,), (1,)))
                top_score = jnp.maximum(top_score, jnp.max(s_lo, axis=1, keepdims=True))
                p_lo = jnp.exp(s_lo - top_score)
            p_hi = jnp.exp(s_hi - top_score)
            total = jnp.sum(p_hi, axis=1, keepdims=True)
            out = mm(p_hi.astype(bf16), values[low:top, :], ((1,), (0,)))
            if low:
                total = total + jnp.sum(p_lo, axis=1, keepdims=True)
                out = out + mm(p_lo.astype(bf16), values[:low, :], ((1,), (0,)))
            mixed.append(out / total)
            lse.append(top_score + jnp.log(total))
        out = jnp.where(lane < HEAD, mixed[0], mixed[1])
        o_ref[rows, :] = out
        lse_ref[rows, :] = jnp.where(lane < HEAD, lse[0], lse[1])
        y_ref[rows, :] = (out * jax.nn.sigmoid(gate_ref[0, rows, :])).astype(bf16)


def prefetch_call(kernel, grid, in_specs, out_specs, out_shape, scratch, cost, name, scalars):
    return pl.pallas_call(
        kernel,
        out_shape=out_shape,
        grid_spec=pltpu.PrefetchScalarGridSpec(
            num_scalar_prefetch=1,
            grid=grid,
            in_specs=in_specs,
            out_specs=out_specs,
            scratch_shapes=scratch,
        ),
        cost_estimate=cost,
        compiler_params=pltpu.CompilerParams(vmem_limit_bytes=VMEM_LIMIT),
        name=name,
    )


def attend(scalars, qk, vg, cum):
    _, length, width = qk.shape
    pairs = width // LANES
    block = (1, length, LANES)
    flat = pl.BlockSpec((length, LANES), lambda p, s: (0, p))
    first = lambda p, s: (s[PIECES], 0, p)
    second = lambda p, s: (1 - s[PIECES], 0, p)
    area = length * length * pairs * 2
    return prefetch_call(
        functools.partial(attend_kernel, length),
        (pairs,),
        [
            pl.BlockSpec(block, first),
            pl.BlockSpec(block, second),
            pl.BlockSpec(block, first),
            pl.BlockSpec(block, second),
            flat,
        ],
        [flat, flat, flat],
        (
            jax.ShapeDtypeStruct((length, width), bf16),
            jax.ShapeDtypeStruct((length, width), f32),
            jax.ShapeDtypeStruct((length, width), f32),
        ),
        [pltpu.VMEM((length, 2 * LANES), bf16)],
        pl.CostEstimate(
            flops=area * 600, bytes_accessed=length * width * 26, transcendentals=area
        ),
        "attend",
        scalars,
    )(scalars, qk, qk, vg, vg, cum)


def attend_back_kernel(
    length, starts_ref, q_ref, k_ref, v_ref, gate_ref, cum_ref, o_ref, lse_ref, dy_ref,
    dq_ref, dk_ref, dv_ref, dgate_ref, dcum_ref, keys, summed, vals, dkeys, dvals, dcol,
):
    starts = [starts_ref[i] for i in range(PIECES)]
    lane_all = lax.broadcasted_iota(jnp.int32, (length, LANES), 1)
    spot_all = lane_all % HEAD
    keys[:, :LANES] = k_ref[0]
    keys[:, LANES:] = jnp.where(
        (spot_all >= 6) & (spot_all < 9), jnp.asarray(1.0, bf16), decay_lanes(cum_ref[...], True)
    )
    for h in range(2):
        summed[h] = jnp.where(lane_all // HEAD == h, k_ref[0], jnp.asarray(1.0, bf16))
    vals[...] = v_ref[0].astype(bf16)
    dkeys[...] = jnp.zeros_like(dkeys)
    dvals[...] = jnp.zeros_like(dvals)
    for i in range(length // BLOCK):
        low, top = block_ranges(i, BLOCK, length)
        rows = slice(low, low + BLOCK)
        lane = lax.broadcasted_iota(jnp.int32, (BLOCK, LANES), 1)
        queries = q_ref[0, rows, :] * jnp.asarray(HEAD**-0.5, bf16)
        aug = decay_lanes(cum_ref[rows, :], False)
        gate = jax.nn.sigmoid(gate_ref[0, rows, :])
        mixed = o_ref[rows, :]
        dy = dy_ref[rows, :].astype(f32)
        dmix = (dy * gate).astype(bf16)
        dgate_ref[rows, :] = (dy * mixed * gate * (1.0 - gate)).astype(bf16)
        lse_parts = split3(-lse_ref[rows, :])
        row = low + lax.broadcasted_iota(jnp.int32, (BLOCK, 1), 0)
        col = low + lax.broadcasted_iota(jnp.int32, (1, top - low), 1)
        lower, allowed = pair_masks(row, col, starts)
        grads, sums = [], []
        for h in range(2):
            mine = (lane // HEAD) == h
            zero = jnp.zeros_like(queries)
            spot = lane % HEAD
            aug_h = jnp.where(mine, aug, zero)
            shifted = aug_h
            for j in range(3):
                shifted = jnp.where(mine & (spot == 6 + j), lse_parts[j], shifted)
            left = jnp.concatenate([jnp.where(mine, queries, zero), shifted], 1)
            dmix_h = jnp.where(mine, dmix, zero)
            plain = jnp.concatenate([left[:, :LANES], aug_h], 1)
            grad_q, delta, kept = None, None, []
            for start, stop in ((0, low), (low, top)):
                if start == stop:
                    continue
                scores = mm(left, keys[start:stop, :], ((1,), (1,)))
                if start == low:
                    decay = mm(aug_h, keys[start:stop, LANES:], ((1,), (1,)))
                    scores = hi_fix(scores, decay, lower, allowed)
                probs = jnp.exp(scores)
                dprobs = mm(dmix_h, vals[start:stop, :], ((1,), (1,)))
                part = jnp.sum(probs * dprobs, axis=1, keepdims=True)
                delta = part if delta is None else delta + part
                kept.append((start, stop, probs, dprobs))
            for start, stop, probs, dprobs in kept:
                dscores = (probs * (dprobs - delta)).astype(bf16)
                part = mm(dscores, summed[h, start:stop, :], ((1,), (0,)))
                grad_q = part if grad_q is None else grad_q + part
                dkeys[start:stop, :] += mm(dscores, plain, ((0,), (0,)))
                dvals[start:stop, :] += mm(probs.astype(bf16), dmix_h, ((0,), (0,)))
                if start == low:
                    late = jnp.where(lower, jnp.zeros_like(dscores), dscores)
                    ones = jnp.where(mine, jnp.ones_like(zero), zero)
                    dkeys[start:stop, LANES:] += mm(late, ones * jnp.asarray(-2.0, bf16), ((0,), (0,)))
                    fix = -2.0 * jnp.sum(late.astype(f32), axis=1, keepdims=True)
            grads.append(grad_q)
            sums.append(fix + grad_q[:, (1 - h) * HEAD : (1 - h) * HEAD + 1])
        dq_ref[rows, :] = (jnp.where(lane < HEAD, grads[0], grads[1]) * HEAD**-0.5).astype(bf16)
        dcol[rows, :] = jnp.where(lane < HEAD, sums[0], sums[1])
    dk_ref[...] = dkeys[:, :LANES].astype(bf16)
    dv_ref[...] = dvals[...].astype(bf16)
    cols = dkeys[:, LANES:]
    dcum_ref[...] = dcol[...] - jnp.where(lane_all < HEAD, cols[:, 0:1], cols[:, HEAD : HEAD + 1])


def attend_back(scalars, qk, vg, cum, mixed, lse, dy):
    _, length, width = qk.shape
    pairs = width // LANES
    block = (1, length, LANES)
    flat = pl.BlockSpec((length, LANES), lambda p, s: (0, p))
    first = lambda p, s: (s[PIECES], 0, p)
    second = lambda p, s: (1 - s[PIECES], 0, p)
    area = length * length * pairs * 2
    out = jax.ShapeDtypeStruct((length, width), bf16)
    return prefetch_call(
        functools.partial(attend_back_kernel, length),
        (pairs,),
        [
            pl.BlockSpec(block, first),
            pl.BlockSpec(block, second),
            pl.BlockSpec(block, first),
            pl.BlockSpec(block, second),
            flat,
            flat,
            flat,
            flat,
        ],
        [flat] * 5,
        (out, out, out, out, jax.ShapeDtypeStruct((length, width), f32)),
        [
            pltpu.VMEM((length, 2 * LANES), bf16),
            pltpu.VMEM((2, length, LANES), bf16),
            pltpu.VMEM((length, LANES), bf16),
            pltpu.VMEM((length, 2 * LANES), f32),
            pltpu.VMEM((length, LANES), f32),
            pltpu.VMEM((length, LANES), f32),
        ],
        pl.CostEstimate(
            flops=area * 1500, bytes_accessed=length * width * 34, transcendentals=area
        ),
        "attend_back",
        scalars,
    )(scalars, qk, qk, vg, vg, cum, mixed, lse, dy)


def norm_scale(hidden):
    return lax.rsqrt(jnp.mean(hidden * hidden, axis=-1, keepdims=True) + epsilon)


def norm_back(hidden, inv_rms, gain, grad):
    weighted = grad * gain
    return inv_rms * weighted - hidden * inv_rms**3 * jnp.mean(
        weighted * hidden, axis=-1, keepdims=True
    )


def on_device(
    sizes, tokens_in, cotangent, piece_starts, adapter_ids, gain_att, w_in, w_forget, bias_forget,
    w_out, gain_mlp, w_gate_up, w_down, adapt_in_a, adapt_in_b, adapt_forget_b, adapt_out_a,
    adapt_out_b, adapt_mlp_a, adapt_gu_b, adapt_down_a, adapt_down_b,
):
    nz, ny, nx = sizes
    z, c, y, x = (lax.axis_index(name) for name in "zcyx")
    everyone, fsdp = ("z", "c", "y", "x"), ("z", "c")
    n_fsdp, n_tp = 2 * nz, ny * nx
    count = n_fsdp * n_tp
    rows, depth = tokens_in.shape
    length = rows * nx
    ranks = adapt_out_b.shape[1]
    adapters = ranks // RANK
    d_part = depth // count
    d_fsdp = depth // n_fsdp
    cols_t = w_out.shape[1]
    ff_t = w_down.shape[1]
    heads_t = w_forget.shape[2]
    rank_part = ranks // n_fsdp

    small = jnp.concatenate(
        [
            gain_att[0],
            gain_mlp[0],
            w_forget[0].reshape(-1),
            adapt_forget_b[0].reshape(-1),
            bias_forget[0],
            adapter_ids.astype(bf16),
        ]
    )
    small = lax.all_to_all(
        jnp.broadcast_to(small[None], (count, small.shape[0])), everyone, 0, 0, tiled=True
    )
    cuts = [d_part, d_part, d_fsdp * heads_t, rank_part * heads_t, heads_t, ny]
    at, parts = 0, []
    for cut in cuts:
        parts.append(small[:, at : at + cut])
        at += cut
    gain_a = parts[0].reshape(1, depth).astype(f32)
    gain_m = parts[1].reshape(1, depth).astype(f32)

    def heads_full(part, lead):
        return (
            part.reshape(n_fsdp, n_tp, lead, heads_t).transpose(0, 2, 1, 3).reshape(-1, n_tp * heads_t)
        )

    forget_w = heads_full(parts[2], d_fsdp)
    forget_b = heads_full(parts[3], rank_part)
    forget_bias = parts[4].reshape(n_fsdp, n_tp * heads_t)[:1]
    ids_all = parts[5].reshape(n_fsdp, n_tp, ny)[:, 0].astype(jnp.int32)
    my_id = lax.dynamic_index_in_dim(adapter_ids, y, 0, keepdims=False)
    seq_of = jnp.broadcast_to(ids_all[:, :, None], (n_fsdp, ny, nx)).reshape(count)
    seq_hot = (seq_of[:, None] == jnp.arange(adapters)[None, :]).astype(bf16)

    def z_gather(value, axis):
        return assemble([shift(value, "z", nz, d) if d else value for d in range(nz)], z, axis)

    def core_split(half0, half1):
        keep, send = jnp.where(c == 0, half0, half1), jnp.where(c == 0, half1, half0)
        got = shift(send, "c", 2, 1)
        axis = keep.ndim - 2
        return jnp.where(
            c == 0, jnp.concatenate([keep, got], axis), jnp.concatenate([got, keep], axis)
        )

    def other_core(value):
        return shift(value, "c", 2, 1)

    w4 = w_in[0]
    half0 = jnp.stack([w4[:, 0], w4[:, 2]])
    half1 = jnp.stack([w4[:, 1], w4[:, 3]])
    w4 = core_split(half0, half1)
    chunks = []
    for j in range(2):
        mine = z_gather(w4[j], 0)
        mine = [shift(mine, "y", ny, d) if d else mine for d in range(ny)]
        chunks.append((mine, [other_core(piece) for piece in mine]))

    wo = jnp.swapaxes(w_out[0], 0, 1)
    wo = z_gather(wo[None], 0)
    wo_mine = {}
    for dx in range(nx):
        moved = shift(wo, "x", nx, dx) if dx else wo
        for dy in range(ny):
            wo_mine[dx, dy] = shift(moved, "y", ny, dy) if dy else moved
    wo_keys = [(dx, dy) for dx in range(nx) for dy in range(ny)]
    wo_mine = [wo_mine[key] for key in wo_keys]
    wo_all = out_weight(wo_mine, [other_core(piece) for piece in wo_mine], c)
    wo_all = wo_all.reshape(depth, n_tp * cols_t)

    w3 = jnp.stack([w_gate_up[0][:, 0], w_gate_up[0][:, 1], jnp.swapaxes(w_down[0], 0, 1)])
    w3 = core_split(w3[..., : ff_t // 2], w3[..., ff_t // 2 :])
    n_chunk = max(1, ff_t // 2 // LANES)
    width = ff_t // 2 // n_chunk
    ff_units = []
    for k in range(n_chunk):
        mine = z_gather(w3[..., k * width : (k + 1) * width], 1)
        placed = {}
        if k % 2 == 0:
            for dx in range(nx):
                moved = shift(mine, "x", nx, dx) if dx else mine
                for dy in range(ny):
                    placed[dy, dx] = shift(moved, "y", ny, dy) if dy else moved
        else:
            for dy in range(ny):
                moved = shift(mine, "y", ny, dy) if dy else mine
                for dx in range(nx):
                    placed[dy, dx] = shift(moved, "x", nx, dx) if dx else moved
        order = [placed[dy, dx] for dy in range(ny) for dx in range(nx)]
        ff_units.append((order, [other_core(piece) for piece in order]))

    sub_c, sub_f = cols_t // n_fsdp, ff_t // n_fsdp
    spread = jnp.concatenate(
        [
            adapt_in_b[0].reshape(4, rank_part, n_fsdp, sub_c).transpose(2, 1, 0, 3).reshape(
                n_fsdp, rank_part, 4 * sub_c
            ),
            adapt_out_a[0].reshape(n_fsdp, sub_c, rank_part).transpose(0, 2, 1),
            adapt_gu_b[0].reshape(2, rank_part, n_fsdp, sub_f).transpose(2, 1, 0, 3).reshape(
                n_fsdp, rank_part, 2 * sub_f
            ),
            adapt_down_a[0].reshape(n_fsdp, sub_f, rank_part).transpose(0, 2, 1),
        ],
        axis=2,
    )
    n_cols = spread.shape[2]
    spread = lax.all_to_all(spread, fsdp, 0, 0, tiled=True)
    table_b = spread.reshape(adapters, RANK * n_cols)
    table_a = jnp.concatenate(
        [
            adapt_in_a[0].reshape(d_part, 5, adapters, RANK).transpose(2, 0, 1, 3).reshape(
                adapters, d_part, 5 * RANK
            ),
            adapt_mlp_a[0].reshape(d_part, 2, adapters, RANK).transpose(2, 0, 1, 3).reshape(
                adapters, d_part, 2 * RANK
            ),
            adapt_out_b[0].reshape(adapters, RANK, d_part).transpose(0, 2, 1),
            adapt_down_b[0].reshape(adapters, RANK, d_part).transpose(0, 2, 1),
        ],
        axis=2,
    )
    n_a = d_part * 9 * RANK
    table = jnp.concatenate([table_a.reshape(adapters, n_a), table_b], axis=1)
    chosen = mm(seq_hot, table, ((1,), (0,))).astype(bf16)
    chosen = lax.all_to_all(chosen, everyone, 0, 0, tiled=True)
    map_a = chosen[:, :n_a].reshape(depth, 9 * RANK)
    in_a, mlp_a = map_a[:, : 5 * RANK], map_a[:, 5 * RANK : 7 * RANK]
    out_b, down_b = map_a[:, 7 * RANK : 8 * RANK], map_a[:, 8 * RANK :]

    share = n_fsdp // 2
    r = jnp.arange(count)
    r_c, r_s = r // (share * n_tp), (r // n_tp) % share
    r_y, r_x = (r // nx) % ny, r % nx
    r_true = (((c - r_c) % 2) * share + r_s) * n_tp + ((y - r_y) % ny) * nx + (x - r_x) % nx
    reorder = (r_true[:, None] == r[None, :]).astype(bf16)
    map_b = mm(reorder, chosen[:, n_a:], ((1,), (0,))).astype(bf16)
    map_b = map_b.reshape(2, share, ny, nx, RANK, n_cols)
    cut_b = [4 * sub_c, sub_c, 2 * sub_f, sub_f]
    at, pieces_b = 0, []
    for cut in cut_b:
        pieces_b.append(map_b[..., at : at + cut])
        at += cut
    in_b = pieces_b[0][:, :, :, 0].reshape(2, share, ny, RANK, 4, sub_c)
    half_order_y = in_b.transpose(4, 3, 2, 0, 1, 5)
    in_b = jnp.where(c == 0, half_order_y, jnp.flip(half_order_y, 3)).reshape(4, RANK, ny * cols_t)
    out_a = pieces_b[1].transpose(4, 3, 2, 0, 1, 5)
    out_a = jnp.where(c == 0, out_a, jnp.flip(out_a, 3)).reshape(RANK, n_tp * cols_t)
    per = share // n_chunk
    gu_b = (
        pieces_b[2]
        .reshape(2, n_chunk, per, ny, nx, RANK, 2, sub_f)
        .transpose(1, 3, 4, 6, 5, 0, 2, 7)
        .reshape(n_chunk, n_tp, 2 * RANK, 2 * width)
    )
    down_a = (
        pieces_b[3]
        .reshape(2, n_chunk, per, ny, nx, RANK, sub_f)
        .transpose(1, 3, 4, 5, 0, 2, 6)
        .reshape(n_chunk, n_tp, RANK, 2 * width)
    )
    unit_b = jnp.concatenate([gu_b, down_a, jnp.zeros_like(down_a)], axis=2)

    hidden = tokens_in.astype(f32)
    inv_att = norm_scale(hidden)
    normed = (hidden * inv_att * gain_a).astype(bf16)
    normed_all = in_order([shift(normed, "x", nx, d) if d else normed for d in range(nx)], x, nx)
    low_in = mm(normed_all, in_a, ((1,), (0,))).astype(bf16)
    la = [low_in[:, j * RANK : (j + 1) * RANK] for j in range(5)]
    local_heads = ny * heads_t
    lh = jnp.arange(local_heads)
    true_head = (((y - lh // heads_t) % ny) * nx + x) * heads_t + lh % heads_t
    head_pick = (jnp.arange(n_tp * heads_t)[:, None] == true_head[None, :]).astype(bf16)
    wf = mm(forget_w, head_pick, ((1,), (0,))).astype(bf16)
    bf = mm(forget_b, head_pick, ((1,), (0,))).astype(bf16)
    bf = lax.dynamic_slice_in_dim(bf, my_id * RANK, RANK, 0)
    bias = mm(forget_bias, head_pick, ((1,), (0,)))
    logits = mm(normed_all, wf, ((1,), (0,))) + mm(la[4], bf, ((1,), (0,))) + bias
    log_gate = -jnp.log1p(jnp.exp(-logits))
    order = jnp.arange(length)
    earlier = (order[None, :] <= order[:, None]).astype(bf16)
    cum = mm(earlier, split_columns(log_gate), ((1,), (0,)))
    cum = cum[:, :local_heads] + cum[:, local_heads : 2 * local_heads] + cum[:, 2 * local_heads :]
    cum = jnp.repeat(cum, HEAD, axis=1)

    def core_pick(first, second):
        return jnp.where(c == 0, first, second), jnp.where(c == 0, second, first)

    def project(j, out_type):
        mine, other = chunks[j]
        la_pair = core_pick(la[2 * j], la[2 * j + 1])
        in_b_pair = core_pick(in_b[2 * j], in_b[2 * j + 1])
        out = []
        for pieces, low, up in zip((mine, other), la_pair, in_b_pair):
            weight = jnp.concatenate(pieces, 1)
            out.append(
                (mm(normed_all, weight, ((1,), (0,))) + mm(low, up, ((1,), (0,)))).astype(out_type)
            )
        return jnp.stack(out)

    qk = project(0, bf16)
    vg = project(1, f32)
    my_starts = lax.dynamic_index_in_dim(piece_starts, y, 0, keepdims=False)
    scalars = jnp.concatenate([my_starts, c[None].astype(jnp.int32)])
    merged, mixed, lse = attend(scalars, qk, vg, cum)

    def row_block(value, index):
        return lax.dynamic_slice_in_dim(value, index * rows, rows, 0)

    merged_full = jnp.concatenate(
        [
            shift(row_block(merged, (x + d) % nx), "x", nx, d) if d else row_block(merged, x)
            for d in range(nx)
        ],
        axis=1,
    )
    low_out = mm(merged_full, out_a, ((1,), (1,))).astype(bf16)
    hidden1 = (
        hidden + mm(merged_full, wo_all, ((1,), (1,))) + mm(low_out, out_b, ((1,), (1,)))
    )

    inv_mlp = norm_scale(hidden1)
    normed_m = (hidden1 * inv_mlp * gain_m).astype(bf16)
    low_m = mm(normed_m, mlp_a, ((1,), (0,))).astype(bf16)
    grad_down = mm(cotangent, down_b, ((1,), (0,))).astype(bf16)
    low_all = jnp.concatenate([low_m, grad_down, jnp.zeros_like(grad_down)], axis=1)
    state, unit_grads = None, []
    for k in range(n_chunk):
        own, oth = ff_units[k]
        *state, unit_grad = mlp_call(own, oth, normed_m, cotangent, low_all, unit_b[k], state)
        unit_grads.append(unit_grad)
    ff_out, grad_m, small_m = state
    low_down = small_m[:, 2 * RANK : 3 * RANK].astype(bf16)
    result = (hidden1 + ff_out + mm(low_down, down_b, ((1,), (1,)))).astype(bf16)
    grad_low_m = small_m[:, : 2 * RANK].astype(bf16)
    grad_m = grad_m + mm(grad_low_m, mlp_a, ((1,), (1,)))
    grad1 = cotangent.astype(f32) + norm_back(hidden1, inv_mlp, gain_m, grad_m)

    grad_y = grad1.astype(bf16)
    grad_low_out = mm(grad_y, out_b, ((1,), (0,))).astype(bf16)
    grad_merged = (
        mm(grad_y, wo_all, ((1,), (0,))) + mm(grad_low_out, out_a, ((1,), (0,)))
    ).astype(bf16)
    block = ny * cols_t
    grad_rows = []
    for d in range(nx):
        part = grad_merged[:, d * block : (d + 1) * block]
        grad_rows.append(shift(part, "x", nx, -d) if d else part)
    grad_rows = [grad_rows[-d % nx] for d in range(nx)]
    grad_rows = in_order(grad_rows, x, nx)
    dq, dk, dv, dgate, dcum = attend_back(scalars, qk, vg, cum, mixed, lse, grad_rows)
    dcum = dcum[:, ::HEAD]
    dlog = mm(earlier, split_columns(dcum), ((0,), (0,)))
    dlog = dlog[:, :local_heads] + dlog[:, local_heads : 2 * local_heads] + dlog[:, 2 * local_heads :]
    dforget = (dlog * jax.nn.sigmoid(-logits)).astype(bf16)

    grad_x, grad_la, grad_in_b = 0.0, [], []
    pair_grads = ((dq, dk), (dv, dgate))
    for j in range(2):
        mine, other = chunks[j]
        for pieces, grad in zip((mine, other), core_pick(*pair_grads[j])):
            weight = jnp.concatenate(pieces, 1)
            grad_x = grad_x + mm(grad, weight, ((1,), (1,)))
        for i in range(2):
            grad = pair_grads[j][i]
            grad_la.append(mm(grad, in_b[2 * j + i], ((1,), (1,))))
            grad_in_b.append(mm(la[2 * j + i], grad, ((0,), (0,))))
    grad_x = grad_x + mm(dforget, wf, ((1,), (1,)))
    grad_la.append(mm(dforget, bf, ((1,), (1,))))
    grad_la = jnp.concatenate(grad_la, 1).astype(bf16)
    grad_forget_b = mm(la[4], dforget, ((0,), (0,)))
    grad_x = grad_x.astype(bf16)

    def scatter_rows(value):
        total = row_block(value, x).astype(f32)
        for d in range(1, nx):
            total = total + shift(row_block(value, (x + d) % nx), "x", nx, d).astype(f32)
        return total

    grad_low_in = scatter_rows(grad_la).astype(bf16)
    grad_normed = scatter_rows(grad_x) + mm(grad_low_in, in_a, ((1,), (1,)))
    input_grad = grad1 + norm_back(hidden, inv_att, gain_a, grad_normed)

    part_a = jnp.concatenate(
        [
            mm(normed, grad_low_in, ((0,), (0,))),
            mm(normed_m, grad_low_m, ((0,), (0,))),
            mm(grad_y, low_out, ((0,), (0,))),
            mm(cotangent, low_down, ((0,), (0,))),
        ],
        axis=1,
    ).astype(bf16)
    g_in_b = jnp.stack(grad_in_b).astype(bf16).reshape(4, RANK, ny, 2, share, sub_c)
    g_in_b = jnp.where(c == 0, g_in_b, jnp.flip(g_in_b, 3))
    g_in_b = g_in_b.transpose(3, 4, 2, 1, 0, 5).reshape(2, share, ny, 1, RANK, 4 * sub_c)
    g_in_b = jnp.pad(g_in_b, ((0, 0), (0, 0), (0, 0), (0, nx - 1), (0, 0), (0, 0)))
    g_out_a = mm(grad_low_out, merged_full, ((0,), (0,))).astype(bf16)
    g_out_a = g_out_a.reshape(RANK, nx, ny, 2, share, sub_c)
    g_out_a = jnp.where(c == 0, g_out_a, jnp.flip(g_out_a, 3)).transpose(3, 4, 2, 1, 0, 5)
    g_unit = jnp.stack(unit_grads)
    g_gu_b = (
        g_unit[:, :, : 2 * RANK]
        .reshape(n_chunk, ny, nx, 2, RANK, 2, per, sub_f)
        .transpose(5, 0, 6, 1, 2, 4, 3, 7)
        .reshape(2, share, ny, nx, RANK, 2 * sub_f)
    )
    g_down_a = (
        g_unit[:, :, 2 * RANK : 3 * RANK]
        .reshape(n_chunk, ny, nx, RANK, 2, per, sub_f)
        .transpose(4, 0, 5, 1, 2, 3, 6)
        .reshape(2, share, ny, nx, RANK, sub_f)
    )
    part_b = jnp.concatenate([g_in_b, g_out_a, g_gu_b, g_down_a], axis=-1)
    part_b = mm(reorder, part_b.reshape(count, RANK * n_cols), ((0,), (0,))).astype(bf16)
    part_f = mm(grad_forget_b.astype(bf16), head_pick, ((1,), (1,))).astype(bf16)
    part_f = part_f.reshape(RANK, n_tp, heads_t).transpose(1, 0, 2).reshape(1, n_tp, RANK * heads_t)
    part_f = jnp.broadcast_to(part_f, (n_fsdp, n_tp, RANK * heads_t)).reshape(count, RANK * heads_t)
    sent = jnp.concatenate([part_a.reshape(count, n_a), part_b, part_f], axis=1)
    sent = lax.all_to_all(sent, everyone, 0, 0, tiled=True)
    summed = mm(seq_hot, sent, ((0,), (0,)))
    sum_a = summed[:, :n_a].reshape(adapters, d_part, 9 * RANK)
    n_b = RANK * n_cols
    sum_b = summed[:, n_a : n_a + n_b].reshape(n_fsdp, rank_part, n_cols).astype(bf16)
    sum_f = summed[:, n_a + n_b :].reshape(ranks, heads_t)

    def by_feature(value, blocks):
        value = value.reshape(adapters, d_part, blocks, RANK)
        return value.transpose(1, 2, 0, 3).reshape(1, d_part, blocks * ranks)

    def by_rank(value):
        return value.transpose(0, 2, 1).reshape(1, ranks, d_part)

    out_in_a = by_feature(sum_a[:, :, : 5 * RANK], 5)
    out_mlp_a = by_feature(sum_a[:, :, 5 * RANK : 7 * RANK], 2)
    out_out_b = by_rank(sum_a[:, :, 7 * RANK : 8 * RANK])
    out_down_b = by_rank(sum_a[:, :, 8 * RANK :])
    out_forget = lax.dynamic_slice_in_dim(sum_f, (2 * z + c) * rank_part, rank_part, 0)[None]
    final = lax.all_to_all(sum_b, fsdp, 0, 0, tiled=True).astype(f32)
    at, cuts_b = 0, []
    for cut in cut_b:
        cuts_b.append(final[..., at : at + cut])
        at += cut
    out_in_b = (
        cuts_b[0].reshape(n_fsdp, rank_part, 4, sub_c).transpose(2, 1, 0, 3).reshape(
            1, 4, rank_part, cols_t
        )
    )
    out_out_a = cuts_b[1].transpose(0, 2, 1).reshape(1, cols_t, rank_part)
    out_gu_b = (
        cuts_b[2].reshape(n_fsdp, rank_part, 2, sub_f).transpose(2, 1, 0, 3).reshape(
            1, 2, rank_part, ff_t
        )
    )
    out_down_a = cuts_b[3].transpose(0, 2, 1).reshape(1, ff_t, rank_part)
    return (
        result, input_grad, out_in_a, out_in_b, out_forget, out_out_a, out_out_b, out_mlp_a,
        out_gu_b, out_down_a, out_down_b,
    )


def solution(mesh):
    n_fsdp, n_tp = mesh.shape["fsdp"], mesh.shape["tp"]
    fsdp, tp, both = ("z", "c"), ("y", "x"), ("z", "c", "y", "x")

    def run(*args):
        per_fsdp = args[3].shape[0] // n_fsdp
        sizes = (n_fsdp // 2, per_fsdp, n_tp // per_fsdp)
        devices = mesh.devices.reshape(sizes[0], 2, sizes[1], sizes[2])
        split = Mesh(devices, both)
        return jax.shard_map(
            functools.partial(on_device, sizes),
            mesh=split,
            in_specs=(
                P(both, None),
                P(both, None),
                P(fsdp, None),
                P(fsdp),
                P(None, both),
                P(None, fsdp, None, tp),
                P(None, fsdp, tp),
                P(None, tp),
                P(None, tp, fsdp),
                P(None, both),
                P(None, fsdp, None, tp),
                P(None, tp, fsdp),
                P(None, both, None),
                P(None, None, fsdp, tp),
                P(None, fsdp, tp),
                P(None, tp, fsdp),
                P(None, None, both),
                P(None, both, None),
                P(None, None, fsdp, tp),
                P(None, tp, fsdp),
                P(None, None, both),
            ),
            out_specs=(
                P(both, None),
                P(both, None),
                P(None, both, None),
                P(None, None, fsdp, tp),
                P(None, fsdp, tp),
                P(None, tp, fsdp),
                P(None, None, both),
                P(None, both, None),
                P(None, None, fsdp, tp),
                P(None, tp, fsdp),
                P(None, None, both),
            ),
            check_vma=False,
        )(*args)

    return run
```

```python
import functools

import jax
import jax.numpy as jnp
from jax import lax
from jax.experimental import pallas as pl
from jax.experimental.pallas import tpu as pltpu
from jax.sharding import Mesh, PartitionSpec as P

HEAD = 64
RANK = 16
PIECE = 256
PIECES = 2
LEN = 1024
epsilon = 1e-06
masked_score = -1e30
LANES = 128
BLOCK = 256
VMEM_LIMIT = 60 * 1024 * 1024

f32 = jnp.float32
bf16 = jnp.bfloat16
ANY = pl.BlockSpec(memory_space=pl.ANY)
WHOLE = pl.BlockSpec(memory_space=pltpu.VMEM)


def mm(left, right, dims):
    return lax.dot_general(left, right, ((dims[0], dims[1]), ((), ())), preferred_element_type=f32)


def shift(value, axis, size, step):
    return lax.ppermute(value, axis, [(i, (i + step) % size) for i in range(size)])


def split3(value):
    high = value.astype(bf16)
    rest = value - high.astype(f32)
    mid = rest.astype(bf16)
    low = (rest - mid.astype(f32)).astype(bf16)
    return high, mid, low


def split_columns(value):
    high = lax.reduce_precision(value, 8, 7)
    mid = lax.reduce_precision(value - high, 8, 7)
    return jnp.concatenate([high, mid, value - high - mid], 1).astype(bf16)


def in_order(pieces, index, size, axis=0):
    if size == 1:
        return pieces[0]
    if size == 2:
        return jnp.where(
            index == 0, jnp.concatenate(pieces, axis), jnp.concatenate(pieces[::-1], axis)
        )
    shape = list(pieces[0].shape)
    width = shape[axis]
    shape[axis] = size * width
    out = jnp.zeros(tuple(shape), pieces[0].dtype)
    for d, piece in enumerate(pieces):
        out = lax.dynamic_update_slice_in_dim(out, piece, ((index - d) % size) * width, axis)
    return out


def fetch_rows(gathered, buf, sem, shares, index, columns=None):
    part = gathered.shape[-2]
    for f in range(shares):
        where = pl.ds(f * part, part)
        if columns is None:
            pltpu.make_async_copy(gathered.at[f, index], buf.at[index, where], sem.at[index]).start()
            continue
        for plane, start in enumerate(columns):
            source = gathered.at[f, index, :, pl.ds(start, buf.shape[-1])]
            spot = buf.at[index, plane, where] if len(buf.shape) == 4 else buf.at[index, where]
            pltpu.make_async_copy(source, spot, sem.at[index]).start()


def wait_rows(buf, sem, index):
    pltpu.make_async_copy(buf.at[index], buf.at[index], sem.at[index]).wait()


def project_kernel(shares, blocks, cols, gathered, x_ref, low_ref, up_ref, q_ref, k_ref, v_ref, gate_ref, wbuf, sem):
    for b in range(blocks):
        fetch_rows(gathered, wbuf, sem, shares, b)
    for b in range(blocks):
        wait_rows(wbuf, sem, b)

        def step(i, carry):
            rows = pl.ds(pl.multiple_of(i * BLOCK, BLOCK), BLOCK)
            out = mm(x_ref[rows, :], wbuf[b], ((1,), (0,)))
            out = out + mm(low_ref[rows, :], up_ref[b], ((1,), (0,)))
            for j, ref in enumerate((q_ref, k_ref, v_ref, gate_ref)):
                piece = out[:, j * cols : (j + 1) * cols]
                ref[rows, b * cols : (b + 1) * cols] = piece.astype(ref.dtype)
            return carry

        lax.fori_loop(0, x_ref.shape[0] // BLOCK, step, 0)


def project(gathered, normed, low, up):
    shares, blocks, part, wide = gathered.shape
    length, depth = normed.shape
    cols = wide // 4
    out = jax.ShapeDtypeStruct((length, blocks * cols), bf16)
    return pl.pallas_call(
        functools.partial(project_kernel, shares, blocks, cols),
        out_shape=(out, out, out, jax.ShapeDtypeStruct((length, blocks * cols), f32)),
        in_specs=[ANY] + [WHOLE] * 3,
        out_specs=(WHOLE,) * 4,
        scratch_shapes=[
            pltpu.VMEM((blocks, depth, wide), bf16),
            pltpu.SemaphoreType.DMA((blocks,)),
        ],
        cost_estimate=pl.CostEstimate(
            flops=2 * length * depth * blocks * wide,
            bytes_accessed=2 * depth * blocks * wide + 12 * length * depth,
            transcendentals=0,
        ),
        compiler_params=pltpu.CompilerParams(vmem_limit_bytes=VMEM_LIMIT),
        name="project",
    )(gathered, normed, low, up)


def project_back_kernel(
    shares, blocks, cols, gathered, dq_ref, dk_ref, dv_ref, dgate_ref, tail_ref, wf_ref, low_ref, up_ref,
    dx_ref, dlow_ref, dup_ref, wbuf, sem,
):
    for b in range(blocks):
        fetch_rows(gathered, wbuf, sem, shares, b)
    dup_ref[...] = jnp.zeros_like(dup_ref)
    for b in range(blocks):
        wait_rows(wbuf, sem, b)

    def step(i, carry):
        rows = pl.ds(pl.multiple_of(i * BLOCK, BLOCK), BLOCK)
        total = mm(tail_ref[rows, :], wf_ref[...], ((1,), (1,)))
        small = None
        for b in range(blocks):
            grad = jnp.concatenate(
                [ref[rows, b * cols : (b + 1) * cols] for ref in (dq_ref, dk_ref, dv_ref, dgate_ref)], 1
            )
            total = total + mm(grad, wbuf[b], ((1,), (1,)))
            part = mm(grad, up_ref[b], ((1,), (1,)))
            small = part if small is None else small + part
            dup_ref[b] += mm(low_ref[rows, :], grad, ((0,), (0,)))
        dx_ref[rows, :] = total.astype(bf16)
        dlow_ref[rows, :] = small.astype(bf16)
        return carry

    lax.fori_loop(0, dx_ref.shape[0] // BLOCK, step, 0)


def project_back(gathered, dq, dk, dv, dgate, tail, wf, low, up):
    shares, blocks, part, wide = gathered.shape
    depth, length, ranks = shares * part, dq.shape[0], low.shape[1]
    return pl.pallas_call(
        functools.partial(project_back_kernel, shares, blocks, wide // 4),
        out_shape=(
            jax.ShapeDtypeStruct((length, depth), bf16),
            jax.ShapeDtypeStruct((length, ranks), bf16),
            jax.ShapeDtypeStruct((blocks, ranks, wide), f32),
        ),
        in_specs=[ANY] + [WHOLE] * 8,
        out_specs=(WHOLE,) * 3,
        scratch_shapes=[
            pltpu.VMEM((blocks, depth, wide), bf16),
            pltpu.SemaphoreType.DMA((blocks,)),
        ],
        cost_estimate=pl.CostEstimate(
            flops=2 * length * depth * blocks * wide,
            bytes_accessed=2 * depth * blocks * wide + 8 * length * depth,
            transcendentals=0,
        ),
        compiler_params=pltpu.CompilerParams(vmem_limit_bytes=VMEM_LIMIT),
        name="project_back",
    )(gathered, dq, dk, dv, dgate, tail, wf, low, up)


def out_kernel(shares, ny, nx, cols, start, gathered, base_ref, merged_ref, out_ref, wbuf, sem):
    for b in range(ny * nx):
        fetch_rows(gathered, wbuf, sem, shares, b, (start,))
    out_ref[...] = base_ref[...]
    for b in range(ny * nx):
        wait_rows(wbuf, sem, b)
        at = (b % nx * ny + b // nx) * cols
        out_ref[...] += mm(merged_ref[:, at : at + cols], wbuf[b, :, :cols], ((1,), (1,)))


def out_back_kernel(shares, ny, nx, cols, start, gathered, grad_ref, low_ref, up_ref, out_ref, wbuf, sem):
    for b in range(ny * nx):
        fetch_rows(gathered, wbuf, sem, shares, b, (start,))
    for b in range(ny * nx):
        wait_rows(wbuf, sem, b)
        at = (b % nx * ny + b // nx) * cols
        out = mm(grad_ref[...], wbuf[b, :, :cols], ((1,), (0,)))
        out = out + mm(low_ref[...], up_ref[:, at : at + cols], ((1,), (0,)))
        out_ref[:, at : at + cols] = out.astype(bf16)


def out_call(kernel, sizes, start, gathered, operands, out_shape, name):
    ny, nx, cols = sizes
    shares, blocks, part, total = gathered.shape
    depth = shares * part
    return pl.pallas_call(
        functools.partial(kernel, shares, ny, nx, cols, start),
        out_shape=out_shape,
        in_specs=[ANY] + [WHOLE] * len(operands),
        out_specs=WHOLE,
        scratch_shapes=[
            pltpu.VMEM((blocks, depth, total - start), bf16),
            pltpu.SemaphoreType.DMA((blocks,)),
        ],
        cost_estimate=pl.CostEstimate(
            flops=2 * out_shape.shape[0] * depth * blocks * cols,
            bytes_accessed=2 * depth * blocks * cols + 8 * out_shape.shape[0] * depth,
            transcendentals=0,
        ),
        compiler_params=pltpu.CompilerParams(vmem_limit_bytes=VMEM_LIMIT),
        name=name,
    )(gathered, *operands)


def mlp_kernel(shares, units, first, width, *refs):
    gathered, xm_ref, gz_ref, low_ref, bu_ref = refs[:5]
    refs = refs[5:]
    if not first:
        prior, refs = refs[:3], refs[3:]
    out_ref, dx_ref, small_ref, grad_ref, wbuf, sem = refs
    for u in range(units):
        fetch_rows(gathered, wbuf, sem, shares, u, (0, width, 2 * width))
    if first:
        out_ref[...] = jnp.zeros_like(out_ref)
        dx_ref[...] = jnp.zeros_like(dx_ref)
        small_ref[...] = jnp.zeros_like(small_ref)
    else:
        out_ref[...] = prior[0][...]
        dx_ref[...] = prior[1][...]
        small_ref[...] = prior[2][...]
    low_all = low_ref[...]
    lane = lax.broadcasted_iota(jnp.int32, low_all.shape, 1) // RANK
    zero = jnp.zeros_like(low_all)
    low_e, low_u, low_d = (jnp.where(lane == i, low_all, zero) for i in range(3))

    def step(u, carry):
        wait_rows(wbuf, sem, u)
        bu = bu_ref[u]
        gate = mm(xm_ref[...], wbuf[u, 0], ((1,), (0,))) + mm(low_e, bu, ((1,), (0,)))
        up = mm(xm_ref[...], wbuf[u, 1], ((1,), (0,))) + mm(low_u, bu, ((1,), (0,)))
        dh = mm(gz_ref[...], wbuf[u, 2], ((1,), (0,))) + mm(low_d, bu, ((1,), (0,)))
        sig = jax.nn.sigmoid(gate)
        act = gate * sig
        inner = (act * up).astype(bf16)
        dgate = (dh * up * sig * (1.0 + gate * (1.0 - sig))).astype(bf16)
        dup = (dh * act).astype(bf16)
        out_ref[...] += mm(inner, wbuf[u, 2], ((1,), (1,)))
        dx_ref[...] += mm(dgate, wbuf[u, 0], ((1,), (1,))) + mm(dup, wbuf[u, 1], ((1,), (1,)))
        s_e = mm(dgate, bu, ((1,), (1,)))
        s_u = mm(dup, bu, ((1,), (1,)))
        s_d = mm(inner, bu, ((1,), (1,)))
        small_ref[...] += jnp.where(lane == 0, s_e, jnp.where(lane == 1, s_u, s_d))
        grad_ref[u] = (
            mm(low_e, dgate, ((0,), (0,)))
            + mm(low_u, dup, ((0,), (0,)))
            + mm(low_d, inner, ((0,), (0,)))
        ).astype(bf16)
        return carry

    lax.fori_loop(0, units, step, 0)


def mlp_call(gathered, xm, gz, low, bu, prior):
    shares, units = gathered.shape[:2]
    rows, depth = xm.shape
    width = bu.shape[2]
    first = prior is None
    lanes = low.shape[1]
    flops = units * 2 * rows * depth * width * 6
    return pl.pallas_call(
        functools.partial(mlp_kernel, shares, units, first, width),
        out_shape=(
            jax.ShapeDtypeStruct((rows, depth), f32),
            jax.ShapeDtypeStruct((rows, depth), f32),
            jax.ShapeDtypeStruct((rows, lanes), f32),
            jax.ShapeDtypeStruct((units, lanes, width), bf16),
        ),
        in_specs=[ANY] + [WHOLE] * (4 + (0 if first else 3)),
        out_specs=(WHOLE,) * 4,
        scratch_shapes=[
            pltpu.VMEM((units, 3, depth, width), bf16),
            pltpu.SemaphoreType.DMA((units,)),
        ],
        cost_estimate=pl.CostEstimate(
            flops=flops,
            bytes_accessed=units * 3 * depth * width * 2 + rows * depth * 20,
            transcendentals=units * rows * width,
        ),
        compiler_params=pltpu.CompilerParams(vmem_limit_bytes=VMEM_LIMIT),
        name="feed_forward",
    )(gathered, xm, gz, low, bu, *(() if first else prior))


def decay_lanes(cum, negate):
    high, mid, low = (part.astype(f32) for part in split3(cum))
    lane = lax.broadcasted_iota(jnp.int32, cum.shape, 1) % HEAD
    one = jnp.ones_like(cum)
    if negate:
        picks = (-high, -mid, -low, one, one, one)
    else:
        picks = (one, one, one, high, mid, low)
    out = jnp.zeros_like(cum)
    for i, pick in enumerate(picks):
        out = jnp.where(lane == i, pick, out)
    return out.astype(bf16)


def pair_masks(row, col, starts):
    def label(position, none):
        out = jnp.full(position.shape, none, jnp.int32)
        for i in range(PIECES):
            inside = (position >= starts[i]) & (position < starts[i] + PIECE)
            out = jnp.where(inside, i + 1, out)
        return out

    lower = col <= row
    return lower, lower | (label(row, -1) == label(col, -2))


def hi_fix(scores, decay, lower, allowed):
    return jnp.where(lower, scores, jnp.where(allowed, scores - 2.0 * decay, masked_score))


def block_ranges(i, rows, length):
    low = i * rows
    return low, min(low + rows + PIECE, length)


def attend_kernel(length, starts_ref, q_ref, k_ref, v_ref, gate_ref, cum_ref, y_ref, o_ref, lse_ref, keys):
    starts = [starts_ref[i] for i in range(PIECES)]
    cum = cum_ref[...]
    keys[:, :LANES] = k_ref[...]
    keys[:, LANES:] = decay_lanes(cum, True)
    values = v_ref[...]
    for i in range(length // BLOCK):
        low, top = block_ranges(i, BLOCK, length)
        rows = slice(low, low + BLOCK)
        lane = lax.broadcasted_iota(jnp.int32, (BLOCK, LANES), 1)
        queries = q_ref[rows, :] * jnp.asarray(HEAD**-0.5, bf16)
        aug = decay_lanes(cum_ref[rows, :], False)
        row = low + lax.broadcasted_iota(jnp.int32, (BLOCK, 1), 0)
        col = low + lax.broadcasted_iota(jnp.int32, (1, top - low), 1)
        lower, allowed = pair_masks(row, col, starts)
        mixed, lse = [], []
        for h in range(2):
            mine = (lane // HEAD) == h
            zero = jnp.zeros_like(queries)
            aug_h = jnp.where(mine, aug, zero)
            left = jnp.concatenate([jnp.where(mine, queries, zero), aug_h], 1)
            s_hi = mm(left, keys[low:top, :], ((1,), (1,)))
            decay = mm(aug_h, keys[low:top, LANES:], ((1,), (1,)))
            s_hi = hi_fix(s_hi, decay, lower, allowed)
            top_score = jnp.max(s_hi, axis=1, keepdims=True)
            if low:
                s_lo = mm(left, keys[:low, :], ((1,), (1,)))
                top_score = jnp.maximum(top_score, jnp.max(s_lo, axis=1, keepdims=True))
                p_lo = jnp.exp(s_lo - top_score)
            p_hi = jnp.exp(s_hi - top_score)
            total = jnp.sum(p_hi, axis=1, keepdims=True)
            out = mm(p_hi.astype(bf16), values[low:top, :], ((1,), (0,)))
            if low:
                total = total + jnp.sum(p_lo, axis=1, keepdims=True)
                out = out + mm(p_lo.astype(bf16), values[:low, :], ((1,), (0,)))
            mixed.append(out / total)
            lse.append(top_score + jnp.log(total))
        out = jnp.where(lane < HEAD, mixed[0], mixed[1])
        o_ref[rows, :] = out
        lse_ref[rows, :] = jnp.where(lane < HEAD, lse[0], lse[1])
        y_ref[rows, :] = (out * jax.nn.sigmoid(gate_ref[rows, :])).astype(bf16)


def prefetch_call(kernel, grid, in_specs, out_specs, out_shape, scratch, cost, name, scalars):
    return pl.pallas_call(
        kernel,
        out_shape=out_shape,
        grid_spec=pltpu.PrefetchScalarGridSpec(
            num_scalar_prefetch=1,
            grid=grid,
            in_specs=in_specs,
            out_specs=out_specs,
            scratch_shapes=scratch,
        ),
        cost_estimate=cost,
        compiler_params=pltpu.CompilerParams(vmem_limit_bytes=VMEM_LIMIT),
        name=name,
    )


def attend(scalars, q, k, v, gate, cum):
    length, width = q.shape
    pairs = width // LANES
    flat = pl.BlockSpec((length, LANES), lambda p, s: (0, p))
    area = length * length * pairs * 2
    return prefetch_call(
        functools.partial(attend_kernel, length),
        (pairs,),
        [flat] * 5,
        [flat, flat, flat],
        (
            jax.ShapeDtypeStruct((length, width), bf16),
            jax.ShapeDtypeStruct((length, width), f32),
            jax.ShapeDtypeStruct((length, width), f32),
        ),
        [pltpu.VMEM((length, 2 * LANES), bf16)],
        pl.CostEstimate(
            flops=area * 600, bytes_accessed=length * width * 26, transcendentals=area
        ),
        "attend",
        scalars,
    )(scalars, q, k, v, gate, cum)


def attend_back_kernel(
    length, starts_ref, q_ref, k_ref, v_ref, gate_ref, cum_ref, o_ref, lse_ref, dy_ref,
    dq_ref, dk_ref, dv_ref, dgate_ref, dcum_ref, keys, summed, vals, dkeys, dvals, dcol,
):
    starts = [starts_ref[i] for i in range(PIECES)]
    lane_all = lax.broadcasted_iota(jnp.int32, (length, LANES), 1)
    spot_all = lane_all % HEAD
    keys[:, :LANES] = k_ref[...]
    keys[:, LANES:] = jnp.where(
        (spot_all >= 6) & (spot_all < 9), jnp.asarray(1.0, bf16), decay_lanes(cum_ref[...], True)
    )
    for h in range(2):
        summed[h] = jnp.where(lane_all // HEAD == h, k_ref[...], jnp.asarray(1.0, bf16))
    vals[...] = v_ref[...]
    dkeys[...] = jnp.zeros_like(dkeys)
    dvals[...] = jnp.zeros_like(dvals)
    for i in range(length // BLOCK):
        low, top = block_ranges(i, BLOCK, length)
        rows = slice(low, low + BLOCK)
        lane = lax.broadcasted_iota(jnp.int32, (BLOCK, LANES), 1)
        queries = q_ref[rows, :] * jnp.asarray(HEAD**-0.5, bf16)
        aug = decay_lanes(cum_ref[rows, :], False)
        gate = jax.nn.sigmoid(gate_ref[rows, :])
        mixed = o_ref[rows, :]
        dy = dy_ref[rows, :].astype(f32)
        dmix = (dy * gate).astype(bf16)
        dgate_ref[rows, :] = (dy * mixed * gate * (1.0 - gate)).astype(bf16)
        lse_parts = split3(-lse_ref[rows, :])
        row = low + lax.broadcasted_iota(jnp.int32, (BLOCK, 1), 0)
        col = low + lax.broadcasted_iota(jnp.int32, (1, top - low), 1)
        lower, allowed = pair_masks(row, col, starts)
        grads, sums = [], []
        for h in range(2):
            mine = (lane // HEAD) == h
            zero = jnp.zeros_like(queries)
            spot = lane % HEAD
            aug_h = jnp.where(mine, aug, zero)
            shifted = aug_h
            for j in range(3):
                shifted = jnp.where(mine & (spot == 6 + j), lse_parts[j], shifted)
            left = jnp.concatenate([jnp.where(mine, queries, zero), shifted], 1)
            dmix_h = jnp.where(mine, dmix, zero)
            plain = jnp.concatenate([left[:, :LANES], aug_h], 1)
            grad_q, delta, kept = None, None, []
            for start, stop in ((0, low), (low, top)):
                if start == stop:
                    continue
                scores = mm(left, keys[start:stop, :], ((1,), (1,)))
                if start == low:
                    decay = mm(aug_h, keys[start:stop, LANES:], ((1,), (1,)))
                    scores = hi_fix(scores, decay, lower, allowed)
                probs = jnp.exp(scores)
                dprobs = mm(dmix_h, vals[start:stop, :], ((1,), (1,)))
                part = jnp.sum(probs * dprobs, axis=1, keepdims=True)
                delta = part if delta is None else delta + part
                kept.append((start, stop, probs, dprobs))
            for start, stop, probs, dprobs in kept:
                dscores = (probs * (dprobs - delta)).astype(bf16)
                part = mm(dscores, summed[h, start:stop, :], ((1,), (0,)))
                grad_q = part if grad_q is None else grad_q + part
                dkeys[start:stop, :] += mm(dscores, plain, ((0,), (0,)))
                dvals[start:stop, :] += mm(probs.astype(bf16), dmix_h, ((0,), (0,)))
                if start == low:
                    late = jnp.where(lower, jnp.zeros_like(dscores), dscores)
                    ones = jnp.where(mine, jnp.ones_like(zero), zero)
                    dkeys[start:stop, LANES:] += mm(late, ones * jnp.asarray(-2.0, bf16), ((0,), (0,)))
                    fix = -2.0 * jnp.sum(late.astype(f32), axis=1, keepdims=True)
            grads.append(grad_q)
            sums.append(fix + grad_q[:, (1 - h) * HEAD : (1 - h) * HEAD + 1])
        dq_ref[rows, :] = (jnp.where(lane < HEAD, grads[0], grads[1]) * HEAD**-0.5).astype(bf16)
        dcol[rows, :] = jnp.where(lane < HEAD, sums[0], sums[1])
    dk_ref[...] = dkeys[:, :LANES].astype(bf16)
    dv_ref[...] = dvals[...].astype(bf16)
    cols = dkeys[:, LANES:]
    dcum_ref[...] = dcol[...] - jnp.where(lane_all < HEAD, cols[:, 0:1], cols[:, HEAD : HEAD + 1])


def attend_back(scalars, q, k, v, gate, cum, mixed, lse, dy):
    length, width = q.shape
    pairs = width // LANES
    flat = pl.BlockSpec((length, LANES), lambda p, s: (0, p))
    area = length * length * pairs * 2
    out = jax.ShapeDtypeStruct((length, width), bf16)
    return prefetch_call(
        functools.partial(attend_back_kernel, length),
        (pairs,),
        [flat] * 8,
        [flat] * 5,
        (out, out, out, out, jax.ShapeDtypeStruct((length, width), f32)),
        [
            pltpu.VMEM((length, 2 * LANES), bf16),
            pltpu.VMEM((2, length, LANES), bf16),
            pltpu.VMEM((length, LANES), bf16),
            pltpu.VMEM((length, 2 * LANES), f32),
            pltpu.VMEM((length, LANES), f32),
            pltpu.VMEM((length, LANES), f32),
        ],
        pl.CostEstimate(
            flops=area * 1500, bytes_accessed=length * width * 34, transcendentals=area
        ),
        "attend_back",
        scalars,
    )(scalars, q, k, v, gate, cum, mixed, lse, dy)


def norm_scale(hidden):
    return lax.rsqrt(jnp.mean(hidden * hidden, axis=-1, keepdims=True) + epsilon)


def norm_back(hidden, inv_rms, gain, grad):
    weighted = grad * gain
    return inv_rms * weighted - hidden * inv_rms**3 * jnp.mean(
        weighted * hidden, axis=-1, keepdims=True
    )


def on_device(
    sizes, tokens_in, cotangent, piece_starts, adapter_ids, gain_att, w_in, w_forget, bias_forget,
    w_out, gain_mlp, w_gate_up, w_down, adapt_in_a, adapt_in_b, adapt_forget_b, adapt_out_a,
    adapt_out_b, adapt_mlp_a, adapt_gu_b, adapt_down_a, adapt_down_b,
):
    nz, ny, nx = sizes
    z, c, y, x = (lax.axis_index(name) for name in "zcyx")
    everyone, fsdp = ("z", "c", "y", "x"), ("z", "c")
    n_fsdp, n_tp = 2 * nz, ny * nx
    count = n_fsdp * n_tp
    rows, depth = tokens_in.shape
    length = rows * nx
    ranks = adapt_out_b.shape[1]
    adapters = ranks // RANK
    d_part = depth // count
    d_fsdp = depth // n_fsdp
    cols_t = w_out.shape[1]
    ff_t = w_down.shape[1]
    heads_t = w_forget.shape[2]
    rank_part = ranks // n_fsdp

    small = jnp.concatenate(
        [
            gain_att[0],
            gain_mlp[0],
            w_forget[0].reshape(-1),
            adapt_forget_b[0].reshape(-1),
            bias_forget[0],
            adapter_ids.astype(bf16),
        ]
    )
    small = lax.all_to_all(
        jnp.broadcast_to(small[None], (count, small.shape[0])), everyone, 0, 0, tiled=True
    )
    cuts = [d_part, d_part, d_fsdp * heads_t, rank_part * heads_t, heads_t, ny]
    at, parts = 0, []
    for cut in cuts:
        parts.append(small[:, at : at + cut])
        at += cut
    gain_a = parts[0].reshape(1, depth).astype(f32)
    gain_m = parts[1].reshape(1, depth).astype(f32)

    def heads_full(part, lead):
        return (
            part.reshape(n_fsdp, n_tp, lead, heads_t).transpose(0, 2, 1, 3).reshape(-1, n_tp * heads_t)
        )

    forget_w = heads_full(parts[2], d_fsdp)
    forget_b = heads_full(parts[3], rank_part)
    forget_bias = parts[4].reshape(n_fsdp, n_tp * heads_t)[:1]
    ids_all = parts[5].reshape(n_fsdp, n_tp, ny)[:, 0].astype(jnp.int32)
    my_id = lax.dynamic_index_in_dim(adapter_ids, y, 0, keepdims=False)
    seq_of = jnp.broadcast_to(ids_all[:, :, None], (n_fsdp, ny, nx)).reshape(count)
    seq_hot = (seq_of[:, None] == jnp.arange(adapters)[None, :]).astype(bf16)

    tokens_all = in_order(
        [shift(tokens_in, "x", nx, d) if d else tokens_in for d in range(nx)], x, nx
    )
    w_all = lax.all_gather(w_in[0].reshape(d_fsdp, 4 * cols_t), ("z", "c", "y"))
    w_all = w_all.reshape(n_fsdp, ny, d_fsdp, 4 * cols_t)
    n_chunk = max(1, ff_t // (2 * BLOCK))
    width = ff_t // n_chunk
    w_gate, w_up = w_gate_up[0][:, 0], w_gate_up[0][:, 1]
    w_down_t, w_out_t = jnp.swapaxes(w_down[0], 0, 1), jnp.swapaxes(w_out[0], 0, 1)
    w_out_t = jnp.pad(w_out_t, ((0, 0), (0, -cols_t % LANES)))
    ff_chunks = []
    for k in range(n_chunk):
        piece = [part[:, k * width : (k + 1) * width] for part in (w_gate, w_up, w_down_t)]
        piece = jnp.concatenate(piece + ([] if k else [w_out_t]), axis=1)
        piece = lax.all_gather(piece, everyone)
        ff_chunks.append(piece.reshape(n_fsdp, n_tp, d_fsdp, piece.shape[-1]))
    out_sizes, out_start = (ny, nx, cols_t), 3 * width

    sub_c, sub_f = cols_t // n_fsdp, ff_t // n_fsdp
    spread = jnp.concatenate(
        [
            adapt_in_b[0].reshape(4, rank_part, n_fsdp, sub_c).transpose(2, 1, 0, 3).reshape(
                n_fsdp, rank_part, 4 * sub_c
            ),
            adapt_out_a[0].reshape(n_fsdp, sub_c, rank_part).transpose(0, 2, 1),
            adapt_gu_b[0].reshape(2, rank_part, n_fsdp, sub_f).transpose(2, 1, 0, 3).reshape(
                n_fsdp, rank_part, 2 * sub_f
            ),
            adapt_down_a[0].reshape(n_fsdp, sub_f, rank_part).transpose(0, 2, 1),
        ],
        axis=2,
    )
    n_cols = spread.shape[2]
    spread = lax.all_to_all(spread, fsdp, 0, 0, tiled=True)
    table_b = spread.reshape(adapters, RANK * n_cols)
    table_a = jnp.concatenate(
        [
            adapt_in_a[0].reshape(d_part, 5, adapters, RANK).transpose(2, 0, 1, 3).reshape(
                adapters, d_part, 5 * RANK
            ),
            adapt_mlp_a[0].reshape(d_part, 2, adapters, RANK).transpose(2, 0, 1, 3).reshape(
                adapters, d_part, 2 * RANK
            ),
            adapt_out_b[0].reshape(adapters, RANK, d_part).transpose(0, 2, 1),
            adapt_down_b[0].reshape(adapters, RANK, d_part).transpose(0, 2, 1),
        ],
        axis=2,
    )
    n_a = d_part * 9 * RANK
    table = jnp.concatenate([table_a.reshape(adapters, n_a), table_b], axis=1)
    chosen = mm(seq_hot, table, ((1,), (0,))).astype(bf16)
    chosen = lax.all_to_all(chosen, everyone, 0, 0, tiled=True)
    map_a = chosen[:, :n_a].reshape(depth, 9 * RANK)
    in_a, mlp_a = map_a[:, : 5 * RANK], map_a[:, 5 * RANK : 7 * RANK]
    out_b, down_b = map_a[:, 7 * RANK : 8 * RANK], map_a[:, 8 * RANK :]

    map_b = chosen[:, n_a:].reshape(n_fsdp, ny, nx, RANK, n_cols)
    cut_b = [4 * sub_c, sub_c, 2 * sub_f, sub_f]
    at, pieces_b = 0, []
    for cut in cut_b:
        pieces_b.append(map_b[..., at : at + cut])
        at += cut
    in_b = lax.dynamic_index_in_dim(pieces_b[0], x, 2, keepdims=False)
    in_b = in_b.reshape(n_fsdp, ny, RANK, 4, sub_c).transpose(1, 3, 2, 0, 4)
    in_b = in_b.reshape(ny, 4 * RANK, 1, cols_t)
    own_rank = (jnp.arange(4 * RANK)[:, None] // RANK) == jnp.arange(4)[None, :]
    up_in = jnp.where(own_rank[None, :, :, None], in_b, jnp.zeros_like(in_b))
    up_in = up_in.reshape(ny, 4 * RANK, 4 * cols_t)
    out_a = pieces_b[1].transpose(3, 2, 1, 0, 4).reshape(RANK, n_tp * cols_t)
    per = n_fsdp // n_chunk
    gu_b = (
        pieces_b[2]
        .reshape(n_chunk, per, ny, nx, RANK, 2, sub_f)
        .transpose(0, 2, 3, 5, 4, 1, 6)
        .reshape(n_chunk, n_tp, 2 * RANK, width)
    )
    down_a = (
        pieces_b[3]
        .reshape(n_chunk, per, ny, nx, RANK, sub_f)
        .transpose(0, 2, 3, 4, 1, 5)
        .reshape(n_chunk, n_tp, RANK, width)
    )
    unit_b = jnp.concatenate([gu_b, down_a, jnp.zeros_like(down_a)], axis=2)

    hidden = tokens_in.astype(f32)
    inv_att = norm_scale(hidden)
    normed = (hidden * inv_att * gain_a).astype(bf16)
    hidden_all = tokens_all.astype(f32)
    normed_all = (hidden_all * norm_scale(hidden_all) * gain_a).astype(bf16)
    low_in = mm(normed_all, in_a, ((1,), (0,))).astype(bf16)
    la, la_forget = low_in[:, : 4 * RANK], low_in[:, 4 * RANK :]
    local_heads = ny * heads_t
    lh = jnp.arange(local_heads)
    true_head = ((lh // heads_t) * nx + x) * heads_t + lh % heads_t
    head_pick = (jnp.arange(n_tp * heads_t)[:, None] == true_head[None, :]).astype(bf16)
    wf = mm(forget_w, head_pick, ((1,), (0,))).astype(bf16)
    bf = mm(forget_b, head_pick, ((1,), (0,))).astype(bf16)
    bf = lax.dynamic_slice_in_dim(bf, my_id * RANK, RANK, 0)
    bias = mm(forget_bias, head_pick, ((1,), (0,)))
    logits = mm(normed_all, wf, ((1,), (0,))) + mm(la_forget, bf, ((1,), (0,))) + bias
    log_gate = -jnp.log1p(jnp.exp(-logits))
    order = jnp.arange(length)
    earlier = (order[None, :] <= order[:, None]).astype(bf16)
    cum = mm(earlier, split_columns(log_gate), ((1,), (0,)))
    cum = cum[:, :local_heads] + cum[:, local_heads : 2 * local_heads] + cum[:, 2 * local_heads :]
    cum = jnp.repeat(cum, HEAD, axis=1)

    q, k, v, gate = project(w_all, normed_all, la, up_in)
    my_starts = lax.dynamic_index_in_dim(piece_starts, y, 0, keepdims=False)
    merged, mixed, lse = attend(my_starts, q, k, v, gate, cum)

    def row_block(value, index):
        return lax.dynamic_slice_in_dim(value, index * rows, rows, 0)

    merged_full = in_order(
        [
            shift(row_block(merged, (x + d) % nx), "x", nx, d) if d else row_block(merged, x)
            for d in range(nx)
        ],
        x,
        nx,
        1,
    )
    low_out = mm(merged_full, out_a, ((1,), (1,))).astype(bf16)
    hidden1 = out_call(
        out_kernel,
        out_sizes,
        out_start,
        ff_chunks[0],
        (hidden + mm(low_out, out_b, ((1,), (1,))), merged_full),
        jax.ShapeDtypeStruct((rows, depth), f32),
        "out_project",
    )

    inv_mlp = norm_scale(hidden1)
    normed_m = (hidden1 * inv_mlp * gain_m).astype(bf16)
    low_m = mm(normed_m, mlp_a, ((1,), (0,))).astype(bf16)
    grad_down = mm(cotangent, down_b, ((1,), (0,))).astype(bf16)
    low_all = jnp.concatenate([low_m, grad_down, jnp.zeros_like(grad_down)], axis=1)
    state, unit_grads = None, []
    for i in range(n_chunk):
        *state, unit_grad = mlp_call(ff_chunks[i], normed_m, cotangent, low_all, unit_b[i], state)
        unit_grads.append(unit_grad)
    ff_out, grad_m, small_m = state
    low_down = small_m[:, 2 * RANK : 3 * RANK].astype(bf16)
    result = (hidden1 + ff_out + mm(low_down, down_b, ((1,), (1,)))).astype(bf16)
    grad_low_m = small_m[:, : 2 * RANK].astype(bf16)
    grad_m = grad_m + mm(grad_low_m, mlp_a, ((1,), (1,)))
    grad1 = cotangent.astype(f32) + norm_back(hidden1, inv_mlp, gain_m, grad_m)

    grad_y = grad1.astype(bf16)
    grad_low_out = mm(grad_y, out_b, ((1,), (0,))).astype(bf16)
    grad_merged = out_call(
        out_back_kernel,
        out_sizes,
        out_start,
        ff_chunks[0],
        (grad_y, grad_low_out, out_a),
        jax.ShapeDtypeStruct((rows, n_tp * cols_t), bf16),
        "out_project_back",
    )
    block = ny * cols_t
    grad_rows = []
    for d in range(nx):
        part = lax.dynamic_slice_in_dim(grad_merged, ((x + d) % nx) * block, block, 1)
        grad_rows.append(shift(part, "x", nx, d) if d else part)
    grad_rows = in_order(grad_rows, x, nx)
    dq, dk, dv, dgate, dcum = attend_back(my_starts, q, k, v, gate, cum, mixed, lse, grad_rows)
    dcum = dcum[:, ::HEAD]
    dlog = mm(earlier, split_columns(dcum), ((0,), (0,)))
    dlog = dlog[:, :local_heads] + dlog[:, local_heads : 2 * local_heads] + dlog[:, 2 * local_heads :]
    dforget = (dlog * jax.nn.sigmoid(-logits)).astype(bf16)

    lane_pad = ((0, 0), (0, -local_heads % LANES))
    grad_x, grad_la, grad_up = project_back(
        w_all, dq, dk, dv, dgate, jnp.pad(dforget, lane_pad), jnp.pad(wf, lane_pad), la, up_in
    )
    grad_la = jnp.concatenate([grad_la, mm(dforget, bf, ((1,), (1,))).astype(bf16)], 1)
    grad_forget_b = mm(la_forget, dforget, ((0,), (0,)))

    def scatter_rows(value):
        total = row_block(value, x).astype(f32)
        for d in range(1, nx):
            total = total + shift(row_block(value, (x + d) % nx), "x", nx, d).astype(f32)
        return total

    grad_low_in = scatter_rows(grad_la).astype(bf16)
    grad_normed = scatter_rows(grad_x) + mm(grad_low_in, in_a, ((1,), (1,)))
    input_grad = grad1 + norm_back(hidden, inv_att, gain_a, grad_normed)

    part_a = jnp.concatenate(
        [
            mm(normed, grad_low_in, ((0,), (0,))),
            mm(normed_m, grad_low_m, ((0,), (0,))),
            mm(grad_y, low_out, ((0,), (0,))),
            mm(cotangent, low_down, ((0,), (0,))),
        ],
        axis=1,
    ).astype(bf16)
    g_in_b = grad_up.astype(bf16).reshape(ny, 4, RANK, 4, cols_t)
    g_in_b = jnp.stack([g_in_b[:, i, :, i] for i in range(4)]).reshape(4, ny, RANK, n_fsdp, sub_c)
    g_in_b = g_in_b.transpose(3, 1, 2, 0, 4).reshape(n_fsdp, ny, 1, RANK, 4 * sub_c)
    own_x = (jnp.arange(nx) == x)[None, None, :, None, None]
    g_in_b = jnp.where(own_x, g_in_b, jnp.zeros_like(g_in_b))
    g_out_a = mm(grad_low_out, merged_full, ((0,), (0,))).astype(bf16)
    g_out_a = g_out_a.reshape(RANK, nx, ny, n_fsdp, sub_c).transpose(3, 2, 1, 0, 4)
    g_unit = jnp.stack(unit_grads)
    g_gu_b = (
        g_unit[:, :, : 2 * RANK]
        .reshape(n_chunk, ny, nx, 2, RANK, per, sub_f)
        .transpose(0, 5, 1, 2, 4, 3, 6)
        .reshape(n_fsdp, ny, nx, RANK, 2 * sub_f)
    )
    g_down_a = (
        g_unit[:, :, 2 * RANK : 3 * RANK]
        .reshape(n_chunk, ny, nx, RANK, per, sub_f)
        .transpose(0, 4, 1, 2, 3, 5)
        .reshape(n_fsdp, ny, nx, RANK, sub_f)
    )
    part_b = jnp.concatenate([g_in_b, g_out_a, g_gu_b, g_down_a], axis=-1)
    part_b = part_b.reshape(count, RANK * n_cols)
    part_f = mm(grad_forget_b.astype(bf16), head_pick, ((1,), (1,))).astype(bf16)
    part_f = part_f.reshape(RANK, n_tp, heads_t).transpose(1, 0, 2).reshape(1, n_tp, RANK * heads_t)
    part_f = jnp.broadcast_to(part_f, (n_fsdp, n_tp, RANK * heads_t)).reshape(count, RANK * heads_t)
    sent = jnp.concatenate([part_a.reshape(count, n_a), part_b, part_f], axis=1)
    sent = lax.all_to_all(sent, everyone, 0, 0, tiled=True)
    summed = mm(seq_hot, sent, ((0,), (0,)))
    sum_a = summed[:, :n_a].reshape(adapters, d_part, 9 * RANK)
    n_b = RANK * n_cols
    sum_b = summed[:, n_a : n_a + n_b].reshape(n_fsdp, rank_part, n_cols).astype(bf16)
    sum_f = summed[:, n_a + n_b :].reshape(ranks, heads_t)

    def by_feature(value, blocks):
        value = value.reshape(adapters, d_part, blocks, RANK)
        return value.transpose(1, 2, 0, 3).reshape(1, d_part, blocks * ranks)

    def by_rank(value):
        return value.transpose(0, 2, 1).reshape(1, ranks, d_part)

    out_in_a = by_feature(sum_a[:, :, : 5 * RANK], 5)
    out_mlp_a = by_feature(sum_a[:, :, 5 * RANK : 7 * RANK], 2)
    out_out_b = by_rank(sum_a[:, :, 7 * RANK : 8 * RANK])
    out_down_b = by_rank(sum_a[:, :, 8 * RANK :])
    out_forget = lax.dynamic_slice_in_dim(sum_f, (2 * z + c) * rank_part, rank_part, 0)[None]
    final = lax.all_to_all(sum_b, fsdp, 0, 0, tiled=True).astype(f32)
    at, cuts_b = 0, []
    for cut in cut_b:
        cuts_b.append(final[..., at : at + cut])
        at += cut
    out_in_b = (
        cuts_b[0].reshape(n_fsdp, rank_part, 4, sub_c).transpose(2, 1, 0, 3).reshape(
            1, 4, rank_part, cols_t
        )
    )
    out_out_a = cuts_b[1].transpose(0, 2, 1).reshape(1, cols_t, rank_part)
    out_gu_b = (
        cuts_b[2].reshape(n_fsdp, rank_part, 2, sub_f).transpose(2, 1, 0, 3).reshape(
            1, 2, rank_part, ff_t
        )
    )
    out_down_a = cuts_b[3].transpose(0, 2, 1).reshape(1, ff_t, rank_part)
    return (
        result, input_grad, out_in_a, out_in_b, out_forget, out_out_a, out_out_b, out_mlp_a,
        out_gu_b, out_down_a, out_down_b,
    )


def solution(mesh):
    n_fsdp, n_tp = mesh.shape["fsdp"], mesh.shape["tp"]
    fsdp, tp, both = ("z", "c"), ("y", "x"), ("z", "c", "y", "x")

    def run(*args):
        per_fsdp = args[3].shape[0] // n_fsdp
        sizes = (n_fsdp // 2, per_fsdp, n_tp // per_fsdp)
        devices = mesh.devices.reshape(sizes[0], 2, sizes[1], sizes[2])
        split = Mesh(devices, both)
        return jax.shard_map(
            functools.partial(on_device, sizes),
            mesh=split,
            in_specs=(
                P(both, None),
                P(both, None),
                P(fsdp, None),
                P(fsdp),
                P(None, both),
                P(None, fsdp, None, tp),
                P(None, fsdp, tp),
                P(None, tp),
                P(None, tp, fsdp),
                P(None, both),
                P(None, fsdp, None, tp),
                P(None, tp, fsdp),
                P(None, both, None),
                P(None, None, fsdp, tp),
                P(None, fsdp, tp),
                P(None, tp, fsdp),
                P(None, None, both),
                P(None, both, None),
                P(None, None, fsdp, tp),
                P(None, tp, fsdp),
                P(None, None, both),
            ),
            out_specs=(
                P(both, None),
                P(both, None),
                P(None, both, None),
                P(None, None, fsdp, tp),
                P(None, fsdp, tp),
                P(None, tp, fsdp),
                P(None, None, both),
                P(None, both, None),
                P(None, None, fsdp, tp),
                P(None, tp, fsdp),
                P(None, None, both),
            ),
            check_vma=False,
        )(*args)

    return run
```

```python
import functools

import jax
import jax.numpy as jnp
from jax import lax
from jax.experimental import pallas as pl
from jax.experimental.pallas import tpu as pltpu
from jax.sharding import Mesh, PartitionSpec as P

HEAD = 64
RANK = 16
PIECE = 256
PIECES = 2
LEN = 1024
epsilon = 1e-06
masked_score = -1e30
LANES = 128
BLOCK = 256
VMEM_LIMIT = 60 * 1024 * 1024

f32 = jnp.float32
bf16 = jnp.bfloat16
ANY = pl.BlockSpec(memory_space=pl.ANY)
WHOLE = pl.BlockSpec(memory_space=pltpu.VMEM)


def mm(left, right, dims):
    return lax.dot_general(left, right, ((dims[0], dims[1]), ((), ())), preferred_element_type=f32)


def shift(value, axis, size, step):
    return lax.ppermute(value, axis, [(i, (i + step) % size) for i in range(size)])


def split3(value):
    high = value.astype(bf16)
    rest = value - high.astype(f32)
    mid = rest.astype(bf16)
    low = (rest - mid.astype(f32)).astype(bf16)
    return high, mid, low


def split_columns(value):
    high = lax.reduce_precision(value, 8, 7)
    mid = lax.reduce_precision(value - high, 8, 7)
    return jnp.concatenate([high, mid, value - high - mid], 1).astype(bf16)


def in_order(pieces, index, size, axis=0):
    if size == 1:
        return pieces[0]
    if size == 2:
        return jnp.where(
            index == 0, jnp.concatenate(pieces, axis), jnp.concatenate(pieces[::-1], axis)
        )
    shape = list(pieces[0].shape)
    width = shape[axis]
    shape[axis] = size * width
    out = jnp.zeros(tuple(shape), pieces[0].dtype)
    for d, piece in enumerate(pieces):
        out = lax.dynamic_update_slice_in_dim(out, piece, ((index - d) % size) * width, axis)
    return out


def fetch_rows(gathered, buf, sem, shares, index, columns):
    part = gathered.shape[-2]
    for f in range(shares):
        where = pl.ds(f * part, part)
        for plane, start in enumerate(columns):
            source = gathered.at[f, index, :, pl.ds(start, buf.shape[-1])]
            spot = buf.at[index, plane, where] if len(buf.shape) == 4 else buf.at[index, where]
            pltpu.make_async_copy(source, spot, sem.at[index]).start()


def wait_rows(buf, sem, index):
    pltpu.make_async_copy(buf.at[index], buf.at[index], sem.at[index]).wait()


def fetch_placed(place, sources, buf, sem):
    blocks = buf.shape[0]
    nz, part, _ = sources[0].shape
    for dy in range(blocks):
        block = lax.rem(place[2] - dy + blocks, blocks)
        for dc in range(2):
            core = lax.rem(place[1] + dc, 2)
            for dz in range(nz):
                share = 2 * lax.rem(place[0] - dz + nz, nz) + core
                spot = buf.at[block, pl.ds(pl.multiple_of(share * part, part), part)]
                pltpu.make_async_copy(sources[2 * dy + dc].at[dz], spot, sem.at[block]).start()


def project_kernel(blocks, cols, place, *refs):
    sources, refs = refs[: 2 * blocks], refs[2 * blocks :]
    x_ref, low_ref, up_ref, q_ref, k_ref, v_ref, gate_ref, wbuf, sem = refs
    fetch_placed(place, sources, wbuf, sem)
    for b in range(blocks):
        wait_rows(wbuf, sem, b)

        def step(i, carry):
            rows = pl.ds(pl.multiple_of(i * BLOCK, BLOCK), BLOCK)
            out = mm(x_ref[rows, :], wbuf[b], ((1,), (0,)))
            out = out + mm(low_ref[rows, :], up_ref[b], ((1,), (0,)))
            for j, ref in enumerate((q_ref, k_ref, v_ref, gate_ref)):
                piece = out[:, j * cols : (j + 1) * cols]
                ref[rows, b * cols : (b + 1) * cols] = piece.astype(ref.dtype)
            return carry

        lax.fori_loop(0, x_ref.shape[0] // BLOCK, step, 0)


def placed_call(kernel, operands, place, sources, out_shape, flops, moved, name):
    blocks = len(sources) // 2
    nz, part, wide = sources[0].shape
    return pl.pallas_call(
        functools.partial(kernel, blocks, wide // 4),
        out_shape=out_shape,
        grid_spec=pltpu.PrefetchScalarGridSpec(
            num_scalar_prefetch=1,
            grid=(1,),
            in_specs=[ANY] * len(sources) + [WHOLE] * len(operands),
            out_specs=(WHOLE,) * len(out_shape),
            scratch_shapes=[
                pltpu.VMEM((blocks, 2 * nz * part, wide), bf16),
                pltpu.SemaphoreType.DMA((blocks,)),
            ],
        ),
        cost_estimate=pl.CostEstimate(
            flops=flops,
            bytes_accessed=4 * blocks * nz * part * wide + moved,
            transcendentals=0,
        ),
        compiler_params=pltpu.CompilerParams(vmem_limit_bytes=VMEM_LIMIT),
        name=name,
    )(place, *sources, *operands)


def project(place, sources, normed, low, up):
    length, depth = normed.shape
    wide = len(sources) // 2 * sources[0].shape[2]
    out = jax.ShapeDtypeStruct((length, wide // 4), bf16)
    return placed_call(
        project_kernel,
        (normed, low, up),
        place,
        sources,
        (out, out, out, jax.ShapeDtypeStruct((length, wide // 4), f32)),
        2 * length * depth * wide,
        12 * length * depth,
        "project",
    )


def project_back_kernel(blocks, cols, place, *refs):
    sources, refs = refs[: 2 * blocks], refs[2 * blocks :]
    dq_ref, dk_ref, dv_ref, dgate_ref, tail_ref, wf_ref, low_ref, up_ref = refs[:8]
    dx_ref, dlow_ref, dup_ref, wbuf, sem = refs[8:]
    fetch_placed(place, sources, wbuf, sem)
    dup_ref[...] = jnp.zeros_like(dup_ref)
    for b in range(blocks):
        wait_rows(wbuf, sem, b)

    def step(i, carry):
        rows = pl.ds(pl.multiple_of(i * BLOCK, BLOCK), BLOCK)
        total = mm(tail_ref[rows, :], wf_ref[...], ((1,), (1,)))
        small = None
        for b in range(blocks):
            grad = jnp.concatenate(
                [ref[rows, b * cols : (b + 1) * cols] for ref in (dq_ref, dk_ref, dv_ref, dgate_ref)], 1
            )
            total = total + mm(grad, wbuf[b], ((1,), (1,)))
            part = mm(grad, up_ref[b], ((1,), (1,)))
            small = part if small is None else small + part
            dup_ref[b] += mm(low_ref[rows, :], grad, ((0,), (0,)))
        dx_ref[rows, :] = total.astype(bf16)
        dlow_ref[rows, :] = small.astype(bf16)
        return carry

    lax.fori_loop(0, dx_ref.shape[0] // BLOCK, step, 0)


def project_back(place, sources, dq, dk, dv, dgate, tail, wf, low, up):
    length, ranks = low.shape
    depth, blocks, wide = wf.shape[0], len(sources) // 2, sources[0].shape[2]
    return placed_call(
        project_back_kernel,
        (dq, dk, dv, dgate, tail, wf, low, up),
        place,
        sources,
        (
            jax.ShapeDtypeStruct((length, depth), bf16),
            jax.ShapeDtypeStruct((length, ranks), bf16),
            jax.ShapeDtypeStruct((blocks, ranks, wide), f32),
        ),
        2 * length * depth * blocks * wide,
        8 * length * depth,
        "project_back",
    )


def out_kernel(shares, ny, nx, cols, start, gathered, base_ref, merged_ref, out_ref, wbuf, sem):
    for b in range(ny * nx):
        fetch_rows(gathered, wbuf, sem, shares, b, (start,))
    out_ref[...] = base_ref[...]
    for b in range(ny * nx):
        wait_rows(wbuf, sem, b)
        at = (b % nx * ny + b // nx) * cols
        out_ref[...] += mm(merged_ref[:, at : at + cols], wbuf[b, :, :cols], ((1,), (1,)))


def out_back_kernel(shares, ny, nx, cols, start, gathered, grad_ref, low_ref, up_ref, out_ref, wbuf, sem):
    for b in range(ny * nx):
        fetch_rows(gathered, wbuf, sem, shares, b, (start,))
    for b in range(ny * nx):
        wait_rows(wbuf, sem, b)
        at = (b % nx * ny + b // nx) * cols
        out = mm(grad_ref[...], wbuf[b, :, :cols], ((1,), (0,)))
        out = out + mm(low_ref[...], up_ref[:, at : at + cols], ((1,), (0,)))
        out_ref[:, at : at + cols] = out.astype(bf16)


def out_call(kernel, sizes, start, gathered, operands, out_shape, name):
    ny, nx, cols = sizes
    shares, blocks, part, total = gathered.shape
    depth = shares * part
    return pl.pallas_call(
        functools.partial(kernel, shares, ny, nx, cols, start),
        out_shape=out_shape,
        in_specs=[ANY] + [WHOLE] * len(operands),
        out_specs=WHOLE,
        scratch_shapes=[
            pltpu.VMEM((blocks, depth, total - start), bf16),
            pltpu.SemaphoreType.DMA((blocks,)),
        ],
        cost_estimate=pl.CostEstimate(
            flops=2 * out_shape.shape[0] * depth * blocks * cols,
            bytes_accessed=2 * depth * blocks * cols + 8 * out_shape.shape[0] * depth,
            transcendentals=0,
        ),
        compiler_params=pltpu.CompilerParams(vmem_limit_bytes=VMEM_LIMIT),
        name=name,
    )(gathered, *operands)


def mlp_kernel(shares, units, first, width, *refs):
    gathered, xm_ref, gz_ref, low_ref, bu_ref = refs[:5]
    refs = refs[5:]
    if not first:
        prior, refs = refs[:3], refs[3:]
    out_ref, dx_ref, small_ref, grad_ref, wbuf, sem = refs
    for u in range(units):
        fetch_rows(gathered, wbuf, sem, shares, u, (0, width, 2 * width))
    if first:
        out_ref[...] = jnp.zeros_like(out_ref)
        dx_ref[...] = jnp.zeros_like(dx_ref)
        small_ref[...] = jnp.zeros_like(small_ref)
    else:
        out_ref[...] = prior[0][...]
        dx_ref[...] = prior[1][...]
        small_ref[...] = prior[2][...]
    low_all = low_ref[...]
    lane = lax.broadcasted_iota(jnp.int32, low_all.shape, 1) // RANK
    zero = jnp.zeros_like(low_all)
    low_e, low_u, low_d = (jnp.where(lane == i, low_all, zero) for i in range(3))

    def step(u, carry):
        wait_rows(wbuf, sem, u)
        bu = bu_ref[u]
        gate = mm(xm_ref[...], wbuf[u, 0], ((1,), (0,))) + mm(low_e, bu, ((1,), (0,)))
        up = mm(xm_ref[...], wbuf[u, 1], ((1,), (0,))) + mm(low_u, bu, ((1,), (0,)))
        dh = mm(gz_ref[...], wbuf[u, 2], ((1,), (0,))) + mm(low_d, bu, ((1,), (0,)))
        sig = jax.nn.sigmoid(gate)
        act = gate * sig
        inner = (act * up).astype(bf16)
        dgate = (dh * up * sig * (1.0 + gate * (1.0 - sig))).astype(bf16)
        dup = (dh * act).astype(bf16)
        out_ref[...] += mm(inner, wbuf[u, 2], ((1,), (1,)))
        dx_ref[...] += mm(dgate, wbuf[u, 0], ((1,), (1,))) + mm(dup, wbuf[u, 1], ((1,), (1,)))
        s_e = mm(dgate, bu, ((1,), (1,)))
        s_u = mm(dup, bu, ((1,), (1,)))
        s_d = mm(inner, bu, ((1,), (1,)))
        small_ref[...] += jnp.where(lane == 0, s_e, jnp.where(lane == 1, s_u, s_d))
        grad_ref[u] = (
            mm(low_e, dgate, ((0,), (0,)))
            + mm(low_u, dup, ((0,), (0,)))
            + mm(low_d, inner, ((0,), (0,)))
        ).astype(bf16)
        return carry

    lax.fori_loop(0, units, step, 0)


def mlp_call(gathered, xm, gz, low, bu, prior):
    shares, units = gathered.shape[:2]
    rows, depth = xm.shape
    width = bu.shape[2]
    first = prior is None
    lanes = low.shape[1]
    flops = units * 2 * rows * depth * width * 6
    return pl.pallas_call(
        functools.partial(mlp_kernel, shares, units, first, width),
        out_shape=(
            jax.ShapeDtypeStruct((rows, depth), f32),
            jax.ShapeDtypeStruct((rows, depth), f32),
            jax.ShapeDtypeStruct((rows, lanes), f32),
            jax.ShapeDtypeStruct((units, lanes, width), bf16),
        ),
        in_specs=[ANY] + [WHOLE] * (4 + (0 if first else 3)),
        out_specs=(WHOLE,) * 4,
        scratch_shapes=[
            pltpu.VMEM((units, 3, depth, width), bf16),
            pltpu.SemaphoreType.DMA((units,)),
        ],
        cost_estimate=pl.CostEstimate(
            flops=flops,
            bytes_accessed=units * 3 * depth * width * 2 + rows * depth * 20,
            transcendentals=units * rows * width,
        ),
        compiler_params=pltpu.CompilerParams(vmem_limit_bytes=VMEM_LIMIT),
        name="feed_forward",
    )(gathered, xm, gz, low, bu, *(() if first else prior))


def decay_lanes(cum, negate):
    high, mid, low = (part.astype(f32) for part in split3(cum))
    lane = lax.broadcasted_iota(jnp.int32, cum.shape, 1) % HEAD
    one = jnp.ones_like(cum)
    if negate:
        picks = (-high, -mid, -low, one, one, one)
    else:
        picks = (one, one, one, high, mid, low)
    out = jnp.zeros_like(cum)
    for i, pick in enumerate(picks):
        out = jnp.where(lane == i, pick, out)
    return out.astype(bf16)


def pair_masks(row, col, starts):
    def label(position, none):
        out = jnp.full(position.shape, none, jnp.int32)
        for i in range(PIECES):
            inside = (position >= starts[i]) & (position < starts[i] + PIECE)
            out = jnp.where(inside, i + 1, out)
        return out

    lower = col <= row
    return lower, lower | (label(row, -1) == label(col, -2))


def hi_fix(scores, decay, lower, allowed):
    return jnp.where(lower, scores, jnp.where(allowed, scores - 2.0 * decay, masked_score))


def block_ranges(i, rows, length):
    low = i * rows
    return low, min(low + rows + PIECE, length)


def attend_kernel(length, starts_ref, q_ref, k_ref, v_ref, gate_ref, cum_ref, y_ref, o_ref, lse_ref, keys):
    starts = [starts_ref[i] for i in range(PIECES)]
    cum = cum_ref[...]
    keys[:, :LANES] = k_ref[...]
    keys[:, LANES:] = decay_lanes(cum, True)
    values = v_ref[...]
    for i in range(length // BLOCK):
        low, top = block_ranges(i, BLOCK, length)
        rows = slice(low, low + BLOCK)
        lane = lax.broadcasted_iota(jnp.int32, (BLOCK, LANES), 1)
        queries = q_ref[rows, :] * jnp.asarray(HEAD**-0.5, bf16)
        aug = decay_lanes(cum_ref[rows, :], False)
        row = low + lax.broadcasted_iota(jnp.int32, (BLOCK, 1), 0)
        col = low + lax.broadcasted_iota(jnp.int32, (1, top - low), 1)
        lower, allowed = pair_masks(row, col, starts)
        mixed, lse = [], []
        for h in range(2):
            mine = (lane // HEAD) == h
            zero = jnp.zeros_like(queries)
            aug_h = jnp.where(mine, aug, zero)
            left = jnp.concatenate([jnp.where(mine, queries, zero), aug_h], 1)
            s_hi = mm(left, keys[low:top, :], ((1,), (1,)))
            decay = mm(aug_h, keys[low:top, LANES:], ((1,), (1,)))
            s_hi = hi_fix(s_hi, decay, lower, allowed)
            top_score = jnp.max(s_hi, axis=1, keepdims=True)
            if low:
                s_lo = mm(left, keys[:low, :], ((1,), (1,)))
                top_score = jnp.maximum(top_score, jnp.max(s_lo, axis=1, keepdims=True))
                p_lo = jnp.exp(s_lo - top_score)
            p_hi = jnp.exp(s_hi - top_score)
            total = jnp.sum(p_hi, axis=1, keepdims=True)
            out = mm(p_hi.astype(bf16), values[low:top, :], ((1,), (0,)))
            if low:
                total = total + jnp.sum(p_lo, axis=1, keepdims=True)
                out = out + mm(p_lo.astype(bf16), values[:low, :], ((1,), (0,)))
            mixed.append(out / total)
            lse.append(top_score + jnp.log(total))
        out = jnp.where(lane < HEAD, mixed[0], mixed[1])
        o_ref[rows, :] = out
        lse_ref[rows, :] = jnp.where(lane < HEAD, lse[0], lse[1])
        y_ref[rows, :] = (out * jax.nn.sigmoid(gate_ref[rows, :])).astype(bf16)


def prefetch_call(kernel, grid, in_specs, out_specs, out_shape, scratch, cost, name, scalars):
    return pl.pallas_call(
        kernel,
        out_shape=out_shape,
        grid_spec=pltpu.PrefetchScalarGridSpec(
            num_scalar_prefetch=1,
            grid=grid,
            in_specs=in_specs,
            out_specs=out_specs,
            scratch_shapes=scratch,
        ),
        cost_estimate=cost,
        compiler_params=pltpu.CompilerParams(vmem_limit_bytes=VMEM_LIMIT),
        name=name,
    )


def attend(scalars, q, k, v, gate, cum):
    length, width = q.shape
    pairs = width // LANES
    flat = pl.BlockSpec((length, LANES), lambda p, s: (0, p))
    area = length * length * pairs * 2
    return prefetch_call(
        functools.partial(attend_kernel, length),
        (pairs,),
        [flat] * 5,
        [flat, flat, flat],
        (
            jax.ShapeDtypeStruct((length, width), bf16),
            jax.ShapeDtypeStruct((length, width), f32),
            jax.ShapeDtypeStruct((length, width), f32),
        ),
        [pltpu.VMEM((length, 2 * LANES), bf16)],
        pl.CostEstimate(
            flops=area * 600, bytes_accessed=length * width * 26, transcendentals=area
        ),
        "attend",
        scalars,
    )(scalars, q, k, v, gate, cum)


def attend_back_kernel(
    length, starts_ref, q_ref, k_ref, v_ref, gate_ref, cum_ref, o_ref, lse_ref, dy_ref,
    dq_ref, dk_ref, dv_ref, dgate_ref, dcum_ref, keys, summed, vals, dkeys, dvals, dcol,
):
    starts = [starts_ref[i] for i in range(PIECES)]
    lane_all = lax.broadcasted_iota(jnp.int32, (length, LANES), 1)
    spot_all = lane_all % HEAD
    keys[:, :LANES] = k_ref[...]
    keys[:, LANES:] = jnp.where(
        (spot_all >= 6) & (spot_all < 9), jnp.asarray(1.0, bf16), decay_lanes(cum_ref[...], True)
    )
    for h in range(2):
        summed[h] = jnp.where(lane_all // HEAD == h, k_ref[...], jnp.asarray(1.0, bf16))
    vals[...] = v_ref[...]
    dkeys[...] = jnp.zeros_like(dkeys)
    dvals[...] = jnp.zeros_like(dvals)
    for i in range(length // BLOCK):
        low, top = block_ranges(i, BLOCK, length)
        rows = slice(low, low + BLOCK)
        lane = lax.broadcasted_iota(jnp.int32, (BLOCK, LANES), 1)
        queries = q_ref[rows, :] * jnp.asarray(HEAD**-0.5, bf16)
        aug = decay_lanes(cum_ref[rows, :], False)
        gate = jax.nn.sigmoid(gate_ref[rows, :])
        mixed = o_ref[rows, :]
        dy = dy_ref[rows, :].astype(f32)
        dmix = (dy * gate).astype(bf16)
        dgate_ref[rows, :] = (dy * mixed * gate * (1.0 - gate)).astype(bf16)
        lse_parts = split3(-lse_ref[rows, :])
        row = low + lax.broadcasted_iota(jnp.int32, (BLOCK, 1), 0)
        col = low + lax.broadcasted_iota(jnp.int32, (1, top - low), 1)
        lower, allowed = pair_masks(row, col, starts)
        grads, sums = [], []
        for h in range(2):
            mine = (lane // HEAD) == h
            zero = jnp.zeros_like(queries)
            spot = lane % HEAD
            aug_h = jnp.where(mine, aug, zero)
            shifted = aug_h
            for j in range(3):
                shifted = jnp.where(mine & (spot == 6 + j), lse_parts[j], shifted)
            left = jnp.concatenate([jnp.where(mine, queries, zero), shifted], 1)
            dmix_h = jnp.where(mine, dmix, zero)
            plain = jnp.concatenate([left[:, :LANES], aug_h], 1)
            grad_q, delta, kept = None, None, []
            for start, stop in ((0, low), (low, top)):
                if start == stop:
                    continue
                scores = mm(left, keys[start:stop, :], ((1,), (1,)))
                if start == low:
                    decay = mm(aug_h, keys[start:stop, LANES:], ((1,), (1,)))
                    scores = hi_fix(scores, decay, lower, allowed)
                probs = jnp.exp(scores)
                dprobs = mm(dmix_h, vals[start:stop, :], ((1,), (1,)))
                part = jnp.sum(probs * dprobs, axis=1, keepdims=True)
                delta = part if delta is None else delta + part
                kept.append((start, stop, probs, dprobs))
            for start, stop, probs, dprobs in kept:
                dscores = (probs * (dprobs - delta)).astype(bf16)
                part = mm(dscores, summed[h, start:stop, :], ((1,), (0,)))
                grad_q = part if grad_q is None else grad_q + part
                dkeys[start:stop, :] += mm(dscores, plain, ((0,), (0,)))
                dvals[start:stop, :] += mm(probs.astype(bf16), dmix_h, ((0,), (0,)))
                if start == low:
                    late = jnp.where(lower, jnp.zeros_like(dscores), dscores)
                    ones = jnp.where(mine, jnp.ones_like(zero), zero)
                    dkeys[start:stop, LANES:] += mm(late, ones * jnp.asarray(-2.0, bf16), ((0,), (0,)))
                    fix = -2.0 * jnp.sum(late.astype(f32), axis=1, keepdims=True)
            grads.append(grad_q)
            sums.append(fix + grad_q[:, (1 - h) * HEAD : (1 - h) * HEAD + 1])
        dq_ref[rows, :] = (jnp.where(lane < HEAD, grads[0], grads[1]) * HEAD**-0.5).astype(bf16)
        dcol[rows, :] = jnp.where(lane < HEAD, sums[0], sums[1])
    dk_ref[...] = dkeys[:, :LANES].astype(bf16)
    dv_ref[...] = dvals[...].astype(bf16)
    cols = dkeys[:, LANES:]
    dcum_ref[...] = dcol[...] - jnp.where(lane_all < HEAD, cols[:, 0:1], cols[:, HEAD : HEAD + 1])


def attend_back(scalars, q, k, v, gate, cum, mixed, lse, dy):
    length, width = q.shape
    pairs = width // LANES
    flat = pl.BlockSpec((length, LANES), lambda p, s: (0, p))
    area = length * length * pairs * 2
    out = jax.ShapeDtypeStruct((length, width), bf16)
    return prefetch_call(
        functools.partial(attend_back_kernel, length),
        (pairs,),
        [flat] * 8,
        [flat] * 5,
        (out, out, out, out, jax.ShapeDtypeStruct((length, width), f32)),
        [
            pltpu.VMEM((length, 2 * LANES), bf16),
            pltpu.VMEM((2, length, LANES), bf16),
            pltpu.VMEM((length, LANES), bf16),
            pltpu.VMEM((length, 2 * LANES), f32),
            pltpu.VMEM((length, LANES), f32),
            pltpu.VMEM((length, LANES), f32),
        ],
        pl.CostEstimate(
            flops=area * 1500, bytes_accessed=length * width * 34, transcendentals=area
        ),
        "attend_back",
        scalars,
    )(scalars, q, k, v, gate, cum, mixed, lse, dy)


def norm_scale(hidden):
    return lax.rsqrt(jnp.mean(hidden * hidden, axis=-1, keepdims=True) + epsilon)


def norm_back(hidden, inv_rms, gain, grad):
    weighted = grad * gain
    return inv_rms * weighted - hidden * inv_rms**3 * jnp.mean(
        weighted * hidden, axis=-1, keepdims=True
    )


def on_device(
    sizes, tokens_in, cotangent, piece_starts, adapter_ids, gain_att, w_in, w_forget, bias_forget,
    w_out, gain_mlp, w_gate_up, w_down, adapt_in_a, adapt_in_b, adapt_forget_b, adapt_out_a,
    adapt_out_b, adapt_mlp_a, adapt_gu_b, adapt_down_a, adapt_down_b,
):
    nz, ny, nx = sizes
    z, c, y, x = (lax.axis_index(name) for name in "zcyx")
    everyone, fsdp = ("z", "c", "y", "x"), ("z", "c")
    n_fsdp, n_tp = 2 * nz, ny * nx
    count = n_fsdp * n_tp
    rows, depth = tokens_in.shape
    length = rows * nx
    ranks = adapt_out_b.shape[1]
    adapters = ranks // RANK
    d_part = depth // count
    d_fsdp = depth // n_fsdp
    cols_t = w_out.shape[1]
    ff_t = w_down.shape[1]
    heads_t = w_forget.shape[2]
    rank_part = ranks // n_fsdp

    small = jnp.concatenate(
        [
            gain_att[0],
            gain_mlp[0],
            w_forget[0].reshape(-1),
            adapt_forget_b[0].reshape(-1),
            bias_forget[0],
            adapter_ids.astype(bf16),
        ]
    )
    small = lax.all_to_all(
        jnp.broadcast_to(small[None], (count, small.shape[0])), everyone, 0, 0, tiled=True
    )
    cuts = [d_part, d_part, d_fsdp * heads_t, rank_part * heads_t, heads_t, ny]
    at, parts = 0, []
    for cut in cuts:
        parts.append(small[:, at : at + cut])
        at += cut
    gain_a = parts[0].reshape(1, depth).astype(f32)
    gain_m = parts[1].reshape(1, depth).astype(f32)

    def heads_full(part, lead):
        return (
            part.reshape(n_fsdp, n_tp, lead, heads_t).transpose(0, 2, 1, 3).reshape(-1, n_tp * heads_t)
        )

    forget_w = heads_full(parts[2], d_fsdp)
    forget_b = heads_full(parts[3], rank_part)
    forget_bias = parts[4].reshape(n_fsdp, n_tp * heads_t)[:1]
    ids_all = parts[5].reshape(n_fsdp, n_tp, ny)[:, 0].astype(jnp.int32)
    my_id = lax.dynamic_index_in_dim(adapter_ids, y, 0, keepdims=False)
    seq_of = jnp.broadcast_to(ids_all[:, :, None], (n_fsdp, ny, nx)).reshape(count)
    seq_hot = (seq_of[:, None] == jnp.arange(adapters)[None, :]).astype(bf16)

    tokens_all = in_order(
        [shift(tokens_in, "x", nx, d) if d else tokens_in for d in range(nx)], x, nx
    )
    w_own = w_in[0].reshape(1, d_fsdp, 4 * cols_t)
    w_own = jnp.concatenate([shift(w_own, "z", nz, d) if d else w_own for d in range(nz)], 0)
    w_all = [shift(w_own, "y", ny, d) if d else w_own for d in range(ny)]
    w_all = [[piece, shift(piece, "c", 2, 1)] for piece in w_all]
    w_all = [piece for pair in w_all for piece in pair]
    place = jnp.stack([z, c, y]).astype(jnp.int32)
    n_chunk = max(1, ff_t // (2 * BLOCK))
    width = ff_t // n_chunk
    w_gate, w_up = w_gate_up[0][:, 0], w_gate_up[0][:, 1]
    w_down_t, w_out_t = jnp.swapaxes(w_down[0], 0, 1), jnp.swapaxes(w_out[0], 0, 1)
    w_out_t = jnp.pad(w_out_t, ((0, 0), (0, -cols_t % LANES)))
    ff_chunks = []
    for k in range(n_chunk):
        piece = [part[:, k * width : (k + 1) * width] for part in (w_gate, w_up, w_down_t)]
        piece = jnp.concatenate(piece + ([] if k else [w_out_t]), axis=1)
        piece = lax.all_gather(piece, everyone)
        ff_chunks.append(piece.reshape(n_fsdp, n_tp, d_fsdp, piece.shape[-1]))
    out_sizes, out_start = (ny, nx, cols_t), 3 * width

    sub_c, sub_f = cols_t // n_fsdp, ff_t // n_fsdp
    spread = jnp.concatenate(
        [
            adapt_in_b[0].reshape(4, rank_part, n_fsdp, sub_c).transpose(2, 1, 0, 3).reshape(
                n_fsdp, rank_part, 4 * sub_c
            ),
            adapt_out_a[0].reshape(n_fsdp, sub_c, rank_part).transpose(0, 2, 1),
            adapt_gu_b[0].reshape(2, rank_part, n_fsdp, sub_f).transpose(2, 1, 0, 3).reshape(
                n_fsdp, rank_part, 2 * sub_f
            ),
            adapt_down_a[0].reshape(n_fsdp, sub_f, rank_part).transpose(0, 2, 1),
        ],
        axis=2,
    )
    n_cols = spread.shape[2]
    spread = lax.all_to_all(spread, fsdp, 0, 0, tiled=True)
    table_b = spread.reshape(adapters, RANK * n_cols)
    table_a = jnp.concatenate(
        [
            adapt_in_a[0].reshape(d_part, 5, adapters, RANK).transpose(2, 0, 1, 3).reshape(
                adapters, d_part, 5 * RANK
            ),
            adapt_mlp_a[0].reshape(d_part, 2, adapters, RANK).transpose(2, 0, 1, 3).reshape(
                adapters, d_part, 2 * RANK
            ),
            adapt_out_b[0].reshape(adapters, RANK, d_part).transpose(0, 2, 1),
            adapt_down_b[0].reshape(adapters, RANK, d_part).transpose(0, 2, 1),
        ],
        axis=2,
    )
    n_a = d_part * 9 * RANK
    table = jnp.concatenate([table_a.reshape(adapters, n_a), table_b], axis=1)
    chosen = mm(seq_hot, table, ((1,), (0,))).astype(bf16)
    chosen = lax.all_to_all(chosen, everyone, 0, 0, tiled=True)
    map_a = chosen[:, :n_a].reshape(depth, 9 * RANK)
    in_a, mlp_a = map_a[:, : 5 * RANK], map_a[:, 5 * RANK : 7 * RANK]
    out_b, down_b = map_a[:, 7 * RANK : 8 * RANK], map_a[:, 8 * RANK :]

    map_b = chosen[:, n_a:].reshape(n_fsdp, ny, nx, RANK, n_cols)
    cut_b = [4 * sub_c, sub_c, 2 * sub_f, sub_f]
    at, pieces_b = 0, []
    for cut in cut_b:
        pieces_b.append(map_b[..., at : at + cut])
        at += cut
    in_b = lax.dynamic_index_in_dim(pieces_b[0], x, 2, keepdims=False)
    in_b = in_b.reshape(n_fsdp, ny, RANK, 4, sub_c).transpose(1, 3, 2, 0, 4)
    in_b = in_b.reshape(ny, 4 * RANK, 1, cols_t)
    own_rank = (jnp.arange(4 * RANK)[:, None] // RANK) == jnp.arange(4)[None, :]
    up_in = jnp.where(own_rank[None, :, :, None], in_b, jnp.zeros_like(in_b))
    up_in = up_in.reshape(ny, 4 * RANK, 4 * cols_t)
    out_a = pieces_b[1].transpose(3, 2, 1, 0, 4).reshape(RANK, n_tp * cols_t)
    per = n_fsdp // n_chunk
    gu_b = (
        pieces_b[2]
        .reshape(n_chunk, per, ny, nx, RANK, 2, sub_f)
        .transpose(0, 2, 3, 5, 4, 1, 6)
        .reshape(n_chunk, n_tp, 2 * RANK, width)
    )
    down_a = (
        pieces_b[3]
        .reshape(n_chunk, per, ny, nx, RANK, sub_f)
        .transpose(0, 2, 3, 4, 1, 5)
        .reshape(n_chunk, n_tp, RANK, width)
    )
    unit_b = jnp.concatenate([gu_b, down_a, jnp.zeros_like(down_a)], axis=2)

    hidden = tokens_in.astype(f32)
    inv_att = norm_scale(hidden)
    normed = (hidden * inv_att * gain_a).astype(bf16)
    hidden_all = tokens_all.astype(f32)
    normed_all = (hidden_all * norm_scale(hidden_all) * gain_a).astype(bf16)
    low_in = mm(normed_all, in_a, ((1,), (0,))).astype(bf16)
    la, la_forget = low_in[:, : 4 * RANK], low_in[:, 4 * RANK :]
    local_heads = ny * heads_t
    lh = jnp.arange(local_heads)
    true_head = ((lh // heads_t) * nx + x) * heads_t + lh % heads_t
    head_pick = (jnp.arange(n_tp * heads_t)[:, None] == true_head[None, :]).astype(bf16)
    wf = mm(forget_w, head_pick, ((1,), (0,))).astype(bf16)
    bf = mm(forget_b, head_pick, ((1,), (0,))).astype(bf16)
    bf = lax.dynamic_slice_in_dim(bf, my_id * RANK, RANK, 0)
    bias = mm(forget_bias, head_pick, ((1,), (0,)))
    logits = mm(normed_all, wf, ((1,), (0,))) + mm(la_forget, bf, ((1,), (0,))) + bias
    log_gate = -jnp.log1p(jnp.exp(-logits))
    order = jnp.arange(length)
    earlier = (order[None, :] <= order[:, None]).astype(bf16)
    cum = mm(earlier, split_columns(log_gate), ((1,), (0,)))
    cum = cum[:, :local_heads] + cum[:, local_heads : 2 * local_heads] + cum[:, 2 * local_heads :]
    cum = jnp.repeat(cum, HEAD, axis=1)

    q, k, v, gate = project(place, w_all, normed_all, la, up_in)
    my_starts = lax.dynamic_index_in_dim(piece_starts, y, 0, keepdims=False)
    merged, mixed, lse = attend(my_starts, q, k, v, gate, cum)

    def row_block(value, index):
        return lax.dynamic_slice_in_dim(value, index * rows, rows, 0)

    merged_full = in_order(
        [
            shift(row_block(merged, (x + d) % nx), "x", nx, d) if d else row_block(merged, x)
            for d in range(nx)
        ],
        x,
        nx,
        1,
    )
    low_out = mm(merged_full, out_a, ((1,), (1,))).astype(bf16)
    hidden1 = out_call(
        out_kernel,
        out_sizes,
        out_start,
        ff_chunks[0],
        (hidden + mm(low_out, out_b, ((1,), (1,))), merged_full),
        jax.ShapeDtypeStruct((rows, depth), f32),
        "out_project",
    )

    inv_mlp = norm_scale(hidden1)
    normed_m = (hidden1 * inv_mlp * gain_m).astype(bf16)
    low_m = mm(normed_m, mlp_a, ((1,), (0,))).astype(bf16)
    grad_down = mm(cotangent, down_b, ((1,), (0,))).astype(bf16)
    low_all = jnp.concatenate([low_m, grad_down, jnp.zeros_like(grad_down)], axis=1)
    state, unit_grads = None, []
    for i in range(n_chunk):
        *state, unit_grad = mlp_call(ff_chunks[i], normed_m, cotangent, low_all, unit_b[i], state)
        unit_grads.append(unit_grad)
    ff_out, grad_m, small_m = state
    low_down = small_m[:, 2 * RANK : 3 * RANK].astype(bf16)
    result = (hidden1 + ff_out + mm(low_down, down_b, ((1,), (1,)))).astype(bf16)
    grad_low_m = small_m[:, : 2 * RANK].astype(bf16)
    grad_m = grad_m + mm(grad_low_m, mlp_a, ((1,), (1,)))
    grad1 = cotangent.astype(f32) + norm_back(hidden1, inv_mlp, gain_m, grad_m)

    grad_y = grad1.astype(bf16)
    grad_low_out = mm(grad_y, out_b, ((1,), (0,))).astype(bf16)
    grad_merged = out_call(
        out_back_kernel,
        out_sizes,
        out_start,
        ff_chunks[0],
        (grad_y, grad_low_out, out_a),
        jax.ShapeDtypeStruct((rows, n_tp * cols_t), bf16),
        "out_project_back",
    )
    block = ny * cols_t
    grad_rows = []
    for d in range(nx):
        part = lax.dynamic_slice_in_dim(grad_merged, ((x + d) % nx) * block, block, 1)
        grad_rows.append(shift(part, "x", nx, d) if d else part)
    grad_rows = in_order(grad_rows, x, nx)
    dq, dk, dv, dgate, dcum = attend_back(my_starts, q, k, v, gate, cum, mixed, lse, grad_rows)
    dcum = dcum[:, ::HEAD]
    dlog = mm(earlier, split_columns(dcum), ((0,), (0,)))
    dlog = dlog[:, :local_heads] + dlog[:, local_heads : 2 * local_heads] + dlog[:, 2 * local_heads :]
    dforget = (dlog * jax.nn.sigmoid(-logits)).astype(bf16)

    lane_pad = ((0, 0), (0, -local_heads % LANES))
    grad_x, grad_la, grad_up = project_back(
        place, w_all, dq, dk, dv, dgate, jnp.pad(dforget, lane_pad), jnp.pad(wf, lane_pad), la, up_in
    )
    grad_la = jnp.concatenate([grad_la, mm(dforget, bf, ((1,), (1,))).astype(bf16)], 1)
    grad_forget_b = mm(la_forget, dforget, ((0,), (0,)))

    def scatter_rows(value):
        total = row_block(value, x).astype(f32)
        for d in range(1, nx):
            total = total + shift(row_block(value, (x + d) % nx), "x", nx, d).astype(f32)
        return total

    grad_low_in = scatter_rows(grad_la).astype(bf16)
    grad_normed = scatter_rows(grad_x) + mm(grad_low_in, in_a, ((1,), (1,)))
    input_grad = grad1 + norm_back(hidden, inv_att, gain_a, grad_normed)

    part_a = jnp.concatenate(
        [
            mm(normed, grad_low_in, ((0,), (0,))),
            mm(normed_m, grad_low_m, ((0,), (0,))),
            mm(grad_y, low_out, ((0,), (0,))),
            mm(cotangent, low_down, ((0,), (0,))),
        ],
        axis=1,
    ).astype(bf16)
    g_in_b = grad_up.astype(bf16).reshape(ny, 4, RANK, 4, cols_t)
    g_in_b = jnp.stack([g_in_b[:, i, :, i] for i in range(4)]).reshape(4, ny, RANK, n_fsdp, sub_c)
    g_in_b = g_in_b.transpose(3, 1, 2, 0, 4).reshape(n_fsdp, ny, 1, RANK, 4 * sub_c)
    own_x = (jnp.arange(nx) == x)[None, None, :, None, None]
    g_in_b = jnp.where(own_x, g_in_b, jnp.zeros_like(g_in_b))
    g_out_a = mm(grad_low_out, merged_full, ((0,), (0,))).astype(bf16)
    g_out_a = g_out_a.reshape(RANK, nx, ny, n_fsdp, sub_c).transpose(3, 2, 1, 0, 4)
    g_unit = jnp.stack(unit_grads)
    g_gu_b = (
        g_unit[:, :, : 2 * RANK]
        .reshape(n_chunk, ny, nx, 2, RANK, per, sub_f)
        .transpose(0, 5, 1, 2, 4, 3, 6)
        .reshape(n_fsdp, ny, nx, RANK, 2 * sub_f)
    )
    g_down_a = (
        g_unit[:, :, 2 * RANK : 3 * RANK]
        .reshape(n_chunk, ny, nx, RANK, per, sub_f)
        .transpose(0, 4, 1, 2, 3, 5)
        .reshape(n_fsdp, ny, nx, RANK, sub_f)
    )
    part_b = jnp.concatenate([g_in_b, g_out_a, g_gu_b, g_down_a], axis=-1)
    part_b = part_b.reshape(count, RANK * n_cols)
    part_f = mm(grad_forget_b.astype(bf16), head_pick, ((1,), (1,))).astype(bf16)
    part_f = part_f.reshape(RANK, n_tp, heads_t).transpose(1, 0, 2).reshape(1, n_tp, RANK * heads_t)
    part_f = jnp.broadcast_to(part_f, (n_fsdp, n_tp, RANK * heads_t)).reshape(count, RANK * heads_t)
    sent = jnp.concatenate([part_a.reshape(count, n_a), part_b, part_f], axis=1)
    sent = lax.all_to_all(sent, everyone, 0, 0, tiled=True)
    summed = mm(seq_hot, sent, ((0,), (0,)))
    sum_a = summed[:, :n_a].reshape(adapters, d_part, 9 * RANK)
    n_b = RANK * n_cols
    sum_b = summed[:, n_a : n_a + n_b].reshape(n_fsdp, rank_part, n_cols).astype(bf16)
    sum_f = summed[:, n_a + n_b :].reshape(ranks, heads_t)

    def by_feature(value, blocks):
        value = value.reshape(adapters, d_part, blocks, RANK)
        return value.transpose(1, 2, 0, 3).reshape(1, d_part, blocks * ranks)

    def by_rank(value):
        return value.transpose(0, 2, 1).reshape(1, ranks, d_part)

    out_in_a = by_feature(sum_a[:, :, : 5 * RANK], 5)
    out_mlp_a = by_feature(sum_a[:, :, 5 * RANK : 7 * RANK], 2)
    out_out_b = by_rank(sum_a[:, :, 7 * RANK : 8 * RANK])
    out_down_b = by_rank(sum_a[:, :, 8 * RANK :])
    out_forget = lax.dynamic_slice_in_dim(sum_f, (2 * z + c) * rank_part, rank_part, 0)[None]
    final = lax.all_to_all(sum_b, fsdp, 0, 0, tiled=True).astype(f32)
    at, cuts_b = 0, []
    for cut in cut_b:
        cuts_b.append(final[..., at : at + cut])
        at += cut
    out_in_b = (
        cuts_b[0].reshape(n_fsdp, rank_part, 4, sub_c).transpose(2, 1, 0, 3).reshape(
            1, 4, rank_part, cols_t
        )
    )
    out_out_a = cuts_b[1].transpose(0, 2, 1).reshape(1, cols_t, rank_part)
    out_gu_b = (
        cuts_b[2].reshape(n_fsdp, rank_part, 2, sub_f).transpose(2, 1, 0, 3).reshape(
            1, 2, rank_part, ff_t
        )
    )
    out_down_a = cuts_b[3].transpose(0, 2, 1).reshape(1, ff_t, rank_part)
    return (
        result, input_grad, out_in_a, out_in_b, out_forget, out_out_a, out_out_b, out_mlp_a,
        out_gu_b, out_down_a, out_down_b,
    )


def solution(mesh):
    n_fsdp, n_tp = mesh.shape["fsdp"], mesh.shape["tp"]
    fsdp, tp, both = ("z", "c"), ("y", "x"), ("z", "c", "y", "x")

    def run(*args):
        per_fsdp = args[3].shape[0] // n_fsdp
        sizes = (n_fsdp // 2, per_fsdp, n_tp // per_fsdp)
        devices = mesh.devices.reshape(sizes[0], 2, sizes[1], sizes[2])
        split = Mesh(devices, both)
        return jax.shard_map(
            functools.partial(on_device, sizes),
            mesh=split,
            in_specs=(
                P(both, None),
                P(both, None),
                P(fsdp, None),
                P(fsdp),
                P(None, both),
                P(None, fsdp, None, tp),
                P(None, fsdp, tp),
                P(None, tp),
                P(None, tp, fsdp),
                P(None, both),
                P(None, fsdp, None, tp),
                P(None, tp, fsdp),
                P(None, both, None),
                P(None, None, fsdp, tp),
                P(None, fsdp, tp),
                P(None, tp, fsdp),
                P(None, None, both),
                P(None, both, None),
                P(None, None, fsdp, tp),
                P(None, tp, fsdp),
                P(None, None, both),
            ),
            out_specs=(
                P(both, None),
                P(both, None),
                P(None, both, None),
                P(None, None, fsdp, tp),
                P(None, fsdp, tp),
                P(None, tp, fsdp),
                P(None, None, both),
                P(None, both, None),
                P(None, None, fsdp, tp),
                P(None, tp, fsdp),
                P(None, None, both),
            ),
            check_vma=False,
        )(*args)

    return run
```
